32 devices in a mesh: req: 4 (over y, core), ad: 8 (over z, x).
Axes of the slice: x: 2, y: 2, z: 4, core: 2. Of those that a mesh axis runs over, the one named last changes fastest.
Arguments:
- residual: bfloat16 [256, 32, 1152], P(('req', 'ad')), may hold values from -16 to 16
- lengths: int32 [256], P(('req', 'ad')), may hold values from 1 to 32, 7168 in all
- adapter_ids: int32 [256], P(('req', 'ad')), may hold values from 0 to 31, as said below
- ffn_gain: float32 [1152], replicated, may hold values from 0.5 to 1.5
- w_gate_up: bfloat16 [2, 1152, 3072], replicated, may hold values from -0.1875 to 0.1875
- w_down: bfloat16 [3072, 1152], replicated, may hold values from -0.109375 to 0.109375
- adapter_input_first: bfloat16 [32, 32, 1152], P('ad'), may hold values from -0.1875 to 0.1875
- ad_out_b: bfloat16 [32, 2, 16, 3072], P('ad'), may hold values from -1.5 to 1.5
- ad_down_a: bfloat16 [32, 16, 3072], P('ad'), may hold values from -0.109375 to 0.109375
- adapter_down_second: bfloat16 [32, 16, 1152], P('ad'), may hold values from -1.5 to 1.5
- final_gain: float32 [1152], replicated, may hold values from 0.5 to 1.5
- head_weight: bfloat16 [1152, 32000], P(None, ('req', 'ad')), may hold values from -3 to 3
Outputs:
- layer_out: bfloat16 [256, 32, 1152], P(('req', 'ad'))
- log_probs: float32 [256, 32000], P(None, ('req', 'ad'))
The draws below stay inside these ranges and needn't reach their ends.
Inputs may be any that keep to these rules, and one draw needn't show every extreme that they name: `adapter_ids`: the 8 requests of one device (aligned blocks of 8 requests in order) use adapters whose indices divided by 4 are all different.
All inputs are finite; a program needn't handle non-finite values. No bound on the sum of `lengths` on one device may be relied on, other than what follows from the above.
Results may differ from the reference program's by a relative error of at most 0.0076.
Values may be sent and summed in bfloat16 or wider, within the bound.
A program may use at most 128 MiB of HBM per device.

```python
import math
import jax
import jax.numpy as jnp
import numpy as np
from jax import lax

D = 1152
FF = 3072
VOCAB = 32000
RANK = 16
AD_DEV = 4
REQ_DEV = 8
SEQ = 32
ADAPTERS = 32
REQS = 256


def draw_residual(key, part):
    rough_key = jax.random.fold_in(jax.random.fold_in(key, 3), 0)
    values = jnp.clip(jax.random.normal(rough_key, (REQS, SEQ, D), jnp.float32), -6.0, 6.0)
    return values.astype(jnp.bfloat16)


def draw_head_weight(key, part):
    entry_key = jax.random.fold_in(jax.random.fold_in(key, 5), 0)
    rising = 0.7 + 0.6 * jnp.arange(VOCAB, dtype=jnp.float32) / VOCAB
    base_scale = 3.0 / math.sqrt(D)
    values = jnp.clip(jax.random.normal(entry_key, (D, VOCAB), jnp.float32), -6.0, 6.0) * (base_scale * rising)[None, :]
    return values.astype(jnp.bfloat16)


def draw_adapter_ids(key, part):
    blocks = REQS // REQ_DEV
    holders = ADAPTERS // AD_DEV
    hot_key, score_key, order_key, used_key = jax.random.split(jax.random.fold_in(key, 9), 4)
    hot = (jax.random.permutation(hot_key, holders) < max(holders // 4, 1)).astype(jnp.int32)
    scores = jax.random.randint(score_key, (blocks, holders), 0, 1024) + 768 * hot[None, :]
    scores = scores * holders + jnp.arange(holders, dtype=jnp.int32)[None, :]
    unused_top, selected_factors = lax.top_k(scores, REQ_DEV)
    shuffle = jax.random.randint(order_key, (blocks, REQ_DEV), 0, 1 << 16) * REQ_DEV + jnp.arange(REQ_DEV, dtype=jnp.int32)[None, :]
    selected_factors = jnp.take_along_axis(selected_factors, jnp.argsort(shuffle, axis=1), axis=1)
    used_local = jax.random.randint(used_key, (blocks, REQ_DEV), 0, AD_DEV)
    named = selected_factors * AD_DEV + used_local
    return named.reshape(REQS).astype(jnp.int32)


def levels(rng, dims, pieces, least, top_value):
    level = 1.0
    for dim, shards_of in pieces:
        draws = jax.random.uniform(jax.random.fold_in(jax.random.fold_in(rng, 6), dim), (shards_of,), jnp.float32, least / len(pieces), top_value / len(pieces))
        level = level * jnp.repeat(jnp.exp(draws), dims[dim] // shards_of).reshape((-1,) + (1,) * (len(dims) - 1 - dim))
    return level


def split_up(number_of, total, bound, lean):
    portions = [(1 << 20) // math.isqrt(rank ** lean) + 1 for rank in range(2, number_of + 1)]
    rest, counts = total - bound - (number_of - 1), [1] * (number_of - 1)
    while rest > 0:
        free = [i for i in range(number_of - 1) if counts[i] < bound]
        whole, remaining = sum([portions[i] for i in free]), rest
        for i in free:
            more = min(bound - counts[i], max(1, remaining * portions[i] // whole), rest)
            counts[i] = counts[i] + more
            rest = rest - more
    return np.array([bound] + counts)


def uneven_parts(key, count, total, reach, skew):
    if count == 2:
        one = jax.random.randint(key, (), max(1, total - reach), min(reach, total - 1) + 1)
        return jnp.stack([one, total - one])
    sizes = jnp.asarray(split_up(count, total, reach, skew), jnp.int32)
    twos = (count - 1) // 2
    source_of, sink = sizes[1:1 + 2 * twos:2], sizes[2:2 + 2 * twos:2]
    margin = jnp.minimum(source_of - 1, reach - sink)
    passed = jax.random.randint(jax.random.fold_in(key, 1), (twos,), 0, 1 << 20) % (margin + 1)
    sizes = sizes.at[1:1 + 2 * twos:2].set(source_of - passed).at[2:2 + 2 * twos:2].set(sink + passed)
    return sizes[jax.random.permutation(jax.random.fold_in(key, 2), count)]


def scatter_about(key, extent, scale, most, cuts=(), kind=jnp.bfloat16):
    loudness = levels(key, extent, cuts, -0.22, 0.18) if cuts else 1.0
    drawn = jax.random.normal(key, extent, jnp.float32) * scale * loudness
    return jnp.minimum(jnp.maximum(drawn, -most), most).astype(kind)


def setup_inputs(seed: int = 0) -> dict:
    arg_keys = jax.random.split(jax.random.key(seed), 13)
    residual = draw_residual(jax.random.fold_in(arg_keys[12], 71), 0)
    lengths = uneven_parts(arg_keys[1], REQS, REQS * SEQ * 7 // 8, SEQ, 0).astype(jnp.int32)
    adapter_ids = draw_adapter_ids(jax.random.fold_in(arg_keys[12], 71), 0)
    ffn_gain = jnp.clip(1.0 + 0.1 * jax.random.normal(arg_keys[3], (D,), jnp.float32), 0.5, 1.5)
    w_gate_up = scatter_about(arg_keys[4], (2, D, FF), D ** -0.5, 0.1875)
    w_down = scatter_about(arg_keys[5], (FF, D), FF ** -0.5, 0.109375)
    adapter_input_first = scatter_about(arg_keys[6], (ADAPTERS, 2 * RANK, D), D ** -0.5, 0.1875, ((0, 8),))
    ad_out_b = scatter_about(arg_keys[7], (ADAPTERS, 2, RANK, FF), RANK ** -0.5, 1.5, ((0, 8),))
    ad_down_a = scatter_about(arg_keys[8], (ADAPTERS, RANK, FF), FF ** -0.5, 0.109375, ((0, 8),))
    adapter_down_second = scatter_about(arg_keys[9], (ADAPTERS, RANK, D), RANK ** -0.5, 1.5, ((0, 8),))
    final_gain = jnp.clip(1.0 + 0.1 * jax.random.normal(arg_keys[10], (D,), jnp.float32), 0.5, 1.5)
    head_weight = draw_head_weight(jax.random.fold_in(arg_keys[12], 71), 0)
    return {"residual": residual, "lengths": lengths, "adapter_ids": adapter_ids, "ffn_gain": ffn_gain, "w_gate_up": w_gate_up, "w_down": w_down, "adapter_input_first": adapter_input_first, "ad_out_b": ad_out_b, "ad_down_a": ad_down_a, "adapter_down_second": adapter_down_second, "final_gain": final_gain, "head_weight": head_weight}


epsilon = 1e-05

def reference(residual, lengths, adapter_ids, ffn_gain, w_gate_up, w_down, adapter_input_first, ad_out_b, ad_down_a, adapter_down_second, final_gain, head_weight):
    block = math.gcd(REQS, 64)
    blocks = REQS // block

    def layer_block(index):
        start = (index * block).astype(jnp.int32)
        stream = lax.dynamic_slice_in_dim(residual, start, block, 0).astype(jnp.float32)
        req_len = lax.dynamic_slice_in_dim(lengths, start, block, 0)
        selected_factors = lax.dynamic_slice_in_dim(adapter_ids, start, block, 0)
        normalized_rows = (stream * lax.rsqrt(lax.optimization_barrier(jnp.mean(stream * stream, axis=-1, keepdims=True)) + epsilon) * ffn_gain).astype(jnp.bfloat16)
        input_lowrank_state = jnp.einsum('foa,fxa->fox', normalized_rows.astype(jnp.float32), adapter_input_first[selected_factors].astype(jnp.float32)).astype(jnp.bfloat16)
        input_lowrank_state = input_lowrank_state.astype(jnp.float32).reshape(block, SEQ, 2, RANK)
        delta_gu = jnp.einsum('bsjk,bjkf->bsjf', input_lowrank_state, ad_out_b[selected_factors].astype(jnp.float32)).astype(jnp.bfloat16)
        delta_gu = lax.optimization_barrier(delta_gu).astype(jnp.float32)
        flat = normalized_rows.reshape(block * SEQ, D)
        gate = jnp.dot(flat, w_gate_up[0], preferred_element_type=jnp.float32).reshape(block, SEQ, FF) + delta_gu[:, :, 0]
        up_part = jnp.dot(flat, w_gate_up[1], preferred_element_type=jnp.float32).reshape(block, SEQ, FF) + delta_gu[:, :, 1]
        hidden = (jax.nn.silu(gate) * up_part).astype(jnp.bfloat16)
        down_lowrank_state = jnp.einsum('bsf,bkf->bsk', hidden.astype(jnp.float32), ad_down_a[selected_factors].astype(jnp.float32)).astype(jnp.bfloat16)
        down_correction = jnp.einsum('rtc,rca->rta', down_lowrank_state.astype(jnp.float32), adapter_down_second[selected_factors].astype(jnp.float32)).astype(jnp.bfloat16)
        down_correction = lax.optimization_barrier(down_correction).astype(jnp.float32)
        base_down = jnp.dot(hidden.reshape(block * SEQ, FF), w_down, preferred_element_type=jnp.float32).reshape(block, SEQ, D)
        mixed = stream + base_down + down_correction
        valid = jnp.arange(SEQ, dtype=jnp.int32)[None, :] < req_len[:, None]
        block_out = jnp.where(valid[:, :, None], mixed, jnp.zeros_like(mixed)).astype(jnp.bfloat16)
        last_index = (req_len - 1).astype(jnp.int32)[:, None, None]
        last_row = jnp.take_along_axis(block_out, last_index, axis=1)[:, 0, :].astype(jnp.float32)
        final = (last_row * lax.rsqrt(lax.optimization_barrier(jnp.mean(last_row * last_row, axis=-1, keepdims=True)) + epsilon) * final_gain).astype(jnp.bfloat16)
        return (block_out, final)
    outputs, finals = lax.map(layer_block, jnp.arange(blocks, dtype=jnp.int32))
    layer_out = outputs.reshape(REQS, SEQ, D)
    finals = finals.reshape(REQS, D)
    logits = jnp.dot(finals, head_weight, preferred_element_type=jnp.float32)
    highest = lax.optimization_barrier(jnp.max(logits, axis=1, keepdims=True))
    shifted = logits - highest
    log_probs = shifted - jnp.log(lax.optimization_barrier(jnp.sum(jnp.exp(shifted), axis=1, keepdims=True)))
    return (layer_out, log_probs)
```

```python
import functools

import jax
import jax.numpy as jnp
from jax import lax
from jax.experimental import pallas as pl
from jax.experimental.pallas import tpu as pltpu
from jax.sharding import PartitionSpec as P

epsilon = 1e-05
CHUNKS = 2
DEPTH = 4
MESH = pl.DeviceIdType.MESH
VMEM_SPEC = pl.BlockSpec(memory_space=pltpu.VMEM)
ANY_SPEC = pl.BlockSpec(memory_space=pl.ANY)
NT = (((1,), (1,)), ((), ()))


def layer_kernel(
    n_q, groups, per_dev, n_req,
    ids_hbm, len_hbm, x_hbm, gain_ref, fgain_ref, wgu_hbm, wd_hbm, ina_hbm, outb_hbm,
    downa_hbm, downb_hbm, wh_hbm,
    out_ref, lt_ref, lse_ref,
    back,
    ids, lens, xs, stage, mstage, recv, mrecv, normed, low_g, low_u, hidden, mixed, y,
    tmp, info, ends, end_normed, end_hidden,
    wgu, wd, ina, outb, downa, downb, wh,
    gathered, stats, own_stats,
    isem, wsem, lsem, rsend, rrecv, msend, mrec, ysend, yrecv,
    asend, arecv, bsend, brecv, csend, crecv, ssend, srecv,
):
    f32 = jnp.float32
    bf16 = jnp.bfloat16
    q = lax.axis_index("req")
    a = lax.axis_index("ad")
    n = n_q * groups
    me = q * groups + a
    seq, width = xs.shape[1:]
    rank = downa.shape[0] // per_dev
    units = wd.shape[0]
    total_req = n * n_req
    per = groups // CHUNKS
    quarter = groups // 4
    own = 3 * quarter
    bits = groups.bit_length() - 1
    pieces_of = width // 128
    tile_f = 1024
    barrier = pltpu.get_barrier_semaphore()

    def target(k):
        t = lax.rem(me + k, n)
        return (lax.div(t, groups), lax.rem(t, groups))

    def each(low_k, high_k, action):
        def body(k, carry):
            action(k)
            return carry
        lax.fori_loop(low_k, high_k, body, 0)

    def partner(p):
        k = lax.rem(p + quarter, groups)
        t = 0
        for b in range(bits):
            u = lax.rem(lax.div(a, 1 << b), 2)
            v = lax.rem(lax.div(k, 1 << b), 2)
            t = t + (u + v - 2 * u * v) * (1 << b)
        return t

    firsts = [
        pltpu.make_async_copy(ids_hbm, ids, isem.at[0]),
        pltpu.make_async_copy(len_hbm, lens, isem.at[1]),
        pltpu.make_async_copy(x_hbm, xs, isem.at[2]),
    ]
    for copy in firsts:
        copy.start()

    each(1, n, lambda k: pl.semaphore_signal(
        barrier, inc=1, device_id=target(k), device_id_type=MESH))

    loads = [
        pltpu.make_async_copy(ina_hbm, ina, wsem.at[0]),
        pltpu.make_async_copy(outb_hbm, outb, wsem.at[1]),
    ]
    tiles = []
    for t in range(units // tile_f):
        cols = pl.ds(t * tile_f, tile_f)
        tiles.append([
            pltpu.make_async_copy(
                wgu_hbm.at[j, :, cols], wgu.at[j, :, cols], wsem.at[2 + 2 * t + j]
            )
            for j in range(2)
        ])
    at = 2 + 2 * (units // tile_f)
    downs = [
        pltpu.make_async_copy(downa_hbm, downa, wsem.at[at]),
        pltpu.make_async_copy(downb_hbm, downb, wsem.at[at + 1]),
        pltpu.make_async_copy(wd_hbm, wd, wsem.at[at + 2]),
    ]
    head_load = pltpu.make_async_copy(wh_hbm, wh, wsem.at[at + 3])
    for copy in firsts:
        copy.wait()
    for copy in loads + [c for pair in tiles for c in pair] + downs + [head_load]:
        copy.start()

    seq_at = lax.broadcasted_iota(jnp.int32, (seq, width), 0)
    tmp[...] = jnp.zeros_like(tmp)

    def fill(p):
        h = partner(p)
        pick = jnp.int32(-1)
        code = jnp.int32(0)
        size = jnp.int32(0)
        for r in range(n_req):
            i = ids[r]
            hit = lax.div(i, per_dev) == h
            pick = jnp.where(hit, r, pick)
            code = jnp.where(hit, lax.rem(i, per_dev), code)
            size = jnp.where(hit, lens[r], size)
        slot = xs[jnp.maximum(pick, 0)]
        stage[p] = slot
        end = jnp.sum(
            jnp.where(seq_at == size - 1, slot.astype(f32), 0.0), axis=0, keepdims=True
        )
        for c in range(pieces_of):
            tmp[c : c + 1, :] = end[:, c * 128 : (c + 1) * 128]
        for c, value in enumerate((code, size, pick)):
            tmp[pieces_of + c : pieces_of + c + 1, :] = jnp.full((1, 128), value).astype(f32)
        mstage[p] = tmp[...].astype(bf16)

    each(0, groups, fill)
    pl.semaphore_wait(barrier, n - 1)

    def row_copy(p):
        return pltpu.make_async_remote_copy(
            src_ref=stage.at[p], dst_ref=recv.at[p],
            send_sem=rsend.at[p], recv_sem=rrecv.at[p],
            device_id=(q, partner(p)), device_id_type=MESH,
        )

    def meta_copy(p):
        return pltpu.make_async_remote_copy(
            src_ref=mstage.at[p], dst_ref=mrecv.at[p],
            send_sem=msend.at[p], recv_sem=mrec.at[p],
            device_id=(q, partner(p)), device_id_type=MESH,
        )

    def back_copy(p):
        return pltpu.make_async_remote_copy(
            src_ref=y.at[p], dst_ref=back.at[a],
            send_sem=ysend.at[p], recv_sem=yrecv.at[p],
            device_id=(q, partner(p)), device_id_type=MESH,
        )

    own_back = pltpu.make_async_copy(y.at[own], back.at[a], lsem)

    def send_rows(p):
        row_copy(p).start()

    def take_rows(p):
        row_copy(p).wait_recv()

    spread = groups // DEPTH
    pairs = n_q // 2
    plane = pairs * spread
    core = lax.rem(q, 2)
    z = lax.div(a, spread)
    x = lax.rem(a, spread)
    column = q * spread + x
    place_me = lax.div(q, 2) * spread + x

    def deep_copy(j):
        return pltpu.make_async_remote_copy(
            src_ref=gathered.at[column, z], dst_ref=gathered.at[column, z],
            send_sem=asend.at[j], recv_sem=arecv.at[j],
            device_id=(q, lax.rem(z + j, DEPTH) * spread + x), device_id_type=MESH,
        )

    def plane_copy(m):
        t = lax.rem(place_me + m, plane)
        return pltpu.make_async_remote_copy(
            src_ref=gathered.at[column], dst_ref=gathered.at[column],
            send_sem=bsend.at[m], recv_sem=brecv.at[m],
            device_id=(2 * lax.div(t, spread) + core, z * spread + lax.rem(t, spread)),
            device_id_type=MESH,
        )

    def pass_on(m):
        t = lax.rem(place_me + plane - m, plane)
        origin = (2 * lax.div(t, spread) + core) * spread + lax.rem(t, spread)
        return pltpu.make_async_remote_copy(
            src_ref=gathered.at[origin], dst_ref=gathered.at[origin],
            send_sem=csend.at[m], recv_sem=crecv.at[m],
            device_id=(q + 1 - 2 * core, a), device_id_type=MESH,
        )

    def start_deep():
        each(1, DEPTH, lambda j: deep_copy(j).start())

    def start_plane():
        each(1, DEPTH, lambda j: deep_copy(j).wait_recv())
        each(1, plane, lambda m: plane_copy(m).start())
        pass_on(0).start()

    def start_pass():
        def relay(m):
            plane_copy(m).wait_recv()
            pass_on(m).start()
        each(1, plane, relay)

    def stat_copy(k):
        return pltpu.make_async_remote_copy(
            src_ref=own_stats, dst_ref=stats.at[me],
            send_sem=ssend.at[k], recv_sem=srecv.at[k],
            device_id=target(k), device_id_type=MESH,
        )

    gain = gain_ref[...].reshape(1, width)
    lane = lax.broadcasted_iota(jnp.int32, (1, per_dev * 2 * rank), 1)
    lane_d = lax.broadcasted_iota(jnp.int32, (1, per_dev * rank), 1)
    group_of = lax.div(lane, 2 * rank).astype(f32)
    group_d = lax.div(lane_d, rank).astype(f32)
    is_gate = lax.rem(lane, 2 * rank) < rank
    row_at = lax.broadcasted_iota(jnp.int32, (seq, width), 0).astype(f32)
    meta_lane = lax.broadcasted_iota(jnp.int32, (1, 128), 1)

    each(0, own, lambda p: meta_copy(p).start())
    each(own + 1, groups, lambda p: meta_copy(p).start())
    each(quarter, per, send_rows)
    each(0, quarter, send_rows)
    mrecv[own] = mstage[own]
    recv[own] = stage[own]

    each(0, own, lambda p: meta_copy(p).wait_recv())
    each(own + 1, groups, lambda p: meta_copy(p).wait_recv())
    for s in range(groups):
        block = mrecv[s].astype(f32)
        for c in range(pieces_of):
            ends[s : s + 1, c * 128 : (c + 1) * 128] = block[c : c + 1, :]
        for c in range(3):
            info[c, s : s + 1, :] = block[pieces_of + c : pieces_of + c + 1, :]
    end_rows = ends[...]
    mean_sq = jnp.mean(end_rows * end_rows, axis=-1, keepdims=True)
    end_normed[...] = (end_rows * lax.rsqrt(mean_sq + epsilon) * gain).astype(bf16)
    for copy in loads:
        copy.wait()
    low = lax.dot_general(end_normed[...], ina[...], NT, preferred_element_type=f32)
    here = group_of == info[0, :, : lane.shape[1]]
    end_g = jnp.where(here & is_gate, low, 0.0).astype(bf16)
    end_u = jnp.where(here & jnp.logical_not(is_gate), low, 0.0).astype(bf16)
    for t in range(units // tile_f):
        cols = pl.ds(t * tile_f, tile_f)
        for copy in tiles[t]:
            copy.wait()
        gate = jnp.dot(end_normed[...], wgu[0, :, cols], preferred_element_type=f32)
        gate = gate + jnp.dot(end_g, outb[:, cols], preferred_element_type=f32)
        up = jnp.dot(end_normed[...], wgu[1, :, cols], preferred_element_type=f32)
        up = up + jnp.dot(end_u, outb[:, cols], preferred_element_type=f32)
        end_hidden[:, cols] = (gate / (1.0 + jnp.exp(-gate)) * up).astype(bf16)
    for copy in downs:
        copy.wait()
    low_d = lax.dot_general(end_hidden[...], downa[...], NT, preferred_element_type=f32)
    low_d = jnp.where(group_d == info[0, :, : lane_d.shape[1]], low_d, 0.0).astype(bf16)
    total = ends[...] + jnp.dot(end_hidden[...], wd[...], preferred_element_type=f32) + jnp.dot(
        low_d, downb[...], preferred_element_type=f32
    )
    rows = jnp.where(info[1, :, 0:1] > 0.0, total, 0.0).astype(bf16).astype(f32)
    mean_sq = jnp.mean(rows * rows, axis=-1, keepdims=True)
    final = rows * lax.rsqrt(mean_sq + epsilon) * fgain_ref[...].reshape(1, width)
    for s in range(groups):
        info[3, s : s + 1, :] = jnp.where(
            meta_lane == 0, (q * groups + partner(s)).astype(f32), info[2, s : s + 1, :]
        )
    gathered[column, z, :, :width] = final.astype(bf16)
    gathered[column, z, :, width:] = info[3].astype(bf16)
    start_deep()

    for chunk in range(CHUNKS):
        mine = range(chunk * per, (chunk + 1) * per)
        if chunk == 0:
            each(0, per, take_rows)
            each(quarter, per, lambda p: row_copy(p).wait_send())
            each(per, own, send_rows)
            each(own + 1, groups, send_rows)
        else:
            each(per, own, take_rows)
            each(own + 1, groups, take_rows)
        for s in mine:
            v = recv[s].astype(f32)
            mean_sq = jnp.mean(v * v, axis=-1, keepdims=True)
            at = (s - chunk * per) * seq
            normed[at : at + seq, :] = (v * lax.rsqrt(mean_sq + epsilon) * gain).astype(bf16)
        low = lax.dot_general(normed[...], ina[...], NT, preferred_element_type=f32)
        for s in mine:
            at = (s - chunk * per) * seq
            here = group_of == info[0, s : s + 1, : lane.shape[1]]
            piece = low[at : at + seq]
            low_g[at : at + seq, :] = jnp.where(here & is_gate, piece, 0.0).astype(bf16)
            low_u[at : at + seq, :] = jnp.where(
                here & jnp.logical_not(is_gate), piece, 0.0
            ).astype(bf16)

        def units_step(j):
            cols = pl.ds(pl.multiple_of(j * tile_f, tile_f), tile_f)
            gate = jnp.dot(normed[...], wgu[0, :, cols], preferred_element_type=f32)
            gate = gate + jnp.dot(low_g[...], outb[:, cols], preferred_element_type=f32)
            up = jnp.dot(normed[...], wgu[1, :, cols], preferred_element_type=f32)
            up = up + jnp.dot(low_u[...], outb[:, cols], preferred_element_type=f32)
            hidden[:, cols] = (gate / (1.0 + jnp.exp(-gate)) * up).astype(bf16)

        each(0, units // tile_f, units_step)
        if chunk == 1:
            start_pass()
        low_d = lax.dot_general(hidden[...], downa[...], NT, preferred_element_type=f32)
        pieces = []
        for s in mine:
            at = (s - chunk * per) * seq
            here = group_d == info[0, s : s + 1, : lane_d.shape[1]]
            pieces.append(jnp.where(here, low_d[at : at + seq], 0.0))
        low_d = jnp.concatenate(pieces, axis=0).astype(bf16)
        mixed[...] = jnp.dot(hidden[...], wd[...], preferred_element_type=f32) + jnp.dot(
            low_d, downb[...], preferred_element_type=f32
        )
        for s in mine:
            at = (s - chunk * per) * seq
            total = recv[s].astype(f32) + mixed[at : at + seq, :]
            y[s] = jnp.where(row_at < info[1, s : s + 1, 0:1], total, 0.0).astype(bf16)
        if chunk == 0:
            each(quarter, per, lambda p: back_copy(p).start())
            each(0, quarter, lambda p: back_copy(p).start())
            start_plane()
        else:
            each(per, own, lambda p: back_copy(p).start())
            each(own + 1, groups, lambda p: back_copy(p).start())
            own_back.start()

    want = lax.broadcasted_iota(jnp.int32, (total_req, n * groups), 0)
    each(0, plane, lambda m: pass_on(m).wait_recv())
    wide = gathered[...].astype(f32).reshape(n * groups, width + 128)
    named = jnp.transpose(wide[:, width:])
    device = named[0:1, :].astype(jnp.int32)
    pick = named[1:2, :].astype(jnp.int32)
    row_id = jnp.where(pick >= 0, device * n_req + pick, -1)
    place = jnp.where(want == row_id, 1.0, 0.0).astype(bf16)
    ordered = jnp.dot(place, wide[:, :width].astype(bf16), preferred_element_type=f32)
    head_load.wait()
    logits = lax.dot_general(wh[...], ordered.astype(bf16), NT, preferred_element_type=f32)
    lt_ref[...] = logits
    top = jnp.max(logits, axis=0, keepdims=True)
    own_stats[0:1, :] = top
    own_stats[1:2, :] = jnp.sum(jnp.exp(logits - top), axis=0, keepdims=True)
    each(1, n, lambda k: stat_copy(k).start())
    stats[me] = own_stats[...]

    def settle(p):
        row_copy(p).wait_send()
        meta_copy(p).wait_send()
        back_copy(p).wait()

    each(0, quarter, settle)

    def settle_far(p):
        meta_copy(p).wait_send()
        back_copy(p).wait()

    each(quarter, per, settle_far)
    each(per, own, settle)
    each(own + 1, groups, settle)
    own_back.wait()
    for r in range(n_req):
        out_ref[r] = back[lax.div(ids[r], per_dev)]
    each(1, DEPTH, lambda j: deep_copy(j).wait_send())
    each(1, plane, lambda m: plane_copy(m).wait_send())
    each(0, plane, lambda m: pass_on(m).wait_send())
    each(1, n, lambda k: stat_copy(k).wait())
    tops = stats[:, 0, :]
    best = jnp.max(tops, axis=0, keepdims=True)
    total = jnp.sum(stats[:, 1, :] * jnp.exp(tops - best), axis=0, keepdims=True)
    lse_ref[...] = best + jnp.log(total)


def finish_kernel(rows_ref, lt_ref, lse_ref, out_ref, lp_ref):
    out_ref[...] = rows_ref[...]
    lp_ref[...] = lt_ref[...] - lse_ref[...]


def finish(rows, logits_t, lse):
    steps = 4
    n_req, seq, width = rows.shape
    shard, total_req = logits_t.shape
    block = pl.cdiv(pl.cdiv(shard, steps), 8) * 8
    row_spec = pl.BlockSpec((n_req // steps, seq, width), lambda i: (i, 0, 0))
    lt_spec = pl.BlockSpec((block, total_req), lambda i: (i, 0))
    return pl.pallas_call(
        finish_kernel,
        out_shape=(
            jax.ShapeDtypeStruct(rows.shape, rows.dtype),
            jax.ShapeDtypeStruct(logits_t.shape, logits_t.dtype),
        ),
        grid=(steps,),
        in_specs=[row_spec, lt_spec, pl.BlockSpec((1, total_req), lambda i: (0, 0))],
        out_specs=(row_spec, lt_spec),
    )(rows, logits_t, lse)


def local(
    residual,
    lengths,
    adapter_ids,
    ffn_gain,
    w_gate_up,
    w_down,
    adapter_input_first,
    ad_out_b,
    ad_down_a,
    adapter_down_second,
    final_gain,
    head_weight,
):
    n_req, seq, width = residual.shape
    groups = lax.axis_size("ad")
    n_q = lax.axis_size("req")
    n = n_q * groups
    per_dev = adapter_input_first.shape[0]
    rank = ad_down_a.shape[1]
    units = w_down.shape[0]
    shard = head_weight.shape[1]
    total_req = n * n_req
    rows = groups // CHUNKS * seq
    plane = n // (2 * DEPTH)
    f32 = jnp.float32
    bf16 = jnp.bfloat16
    ina = adapter_input_first.reshape(per_dev * 2 * rank, width)
    outb = ad_out_b.reshape(per_dev * 2 * rank, units)
    downa = ad_down_a.reshape(per_dev * rank, units)
    downb = adapter_down_second.reshape(per_dev * rank, width)
    head_t = head_weight.T
    dma = pltpu.SemaphoreType.DMA
    vm = pltpu.VMEM
    layer_out, logits_t, lse = pl.pallas_call(
        functools.partial(layer_kernel, n_q, groups, per_dev, n_req),
        out_shape=(
            jax.ShapeDtypeStruct((n_req, seq, width), bf16),
            jax.ShapeDtypeStruct((shard, total_req), f32),
            jax.ShapeDtypeStruct((1, total_req), f32),
        ),
        in_specs=[ANY_SPEC] * 3 + [VMEM_SPEC] * 2 + [ANY_SPEC] * 7,
        out_specs=(VMEM_SPEC,) * 3,
        scratch_shapes=[
            vm((groups, seq, width), bf16),
            pltpu.SMEM((n_req,), jnp.int32),
            pltpu.SMEM((n_req,), jnp.int32),
            vm((n_req, seq, width), bf16),
            vm((groups, seq, width), bf16),
            vm((groups, 16, 128), bf16),
            vm((groups, seq, width), bf16),
            vm((groups, 16, 128), bf16),
            vm((rows, width), bf16),
            vm((rows, per_dev * 2 * rank), bf16),
            vm((rows, per_dev * 2 * rank), bf16),
            vm((rows, units), bf16),
            vm((rows, width), f32),
            vm((groups, seq, width), bf16),
            vm((16, 128), f32),
            vm((4, groups, 128), f32),
            vm((groups, width), f32),
            vm((groups, width), bf16),
            vm((groups, units), bf16),
            vm(w_gate_up.shape, bf16),
            vm(w_down.shape, bf16),
            vm(ina.shape, bf16),
            vm(outb.shape, bf16),
            vm(downa.shape, bf16),
            vm(downb.shape, bf16),
            vm(head_t.shape, bf16),
            vm((n // DEPTH, DEPTH, groups, width + 128), bf16),
            vm((n, 2, total_req), f32),
            vm((2, total_req), f32),
            dma((3,)), dma((12,)), dma(()),
            dma((groups,)), dma((groups,)), dma((groups,)), dma((groups,)),
            dma((groups,)), dma((groups,)),
            dma((DEPTH,)), dma((DEPTH,)),
            dma((plane,)), dma((plane,)), dma((plane,)), dma((plane,)),
            dma((n,)), dma((n,)),
        ],
        compiler_params=pltpu.CompilerParams(
            collective_id=0, has_side_effects=True, vmem_limit_bytes=60 << 20
        ),
    )(
        adapter_ids, lengths, residual, ffn_gain, final_gain, w_gate_up, w_down,
        ina, outb, downa, downb, head_t,
    )
    layer_out, log_probs = finish(layer_out, logits_t, lse)
    return layer_out, log_probs.T


def solution(mesh):
    in_specs = (
        P(("req", "ad"), None, None),
        P(("req", "ad")),
        P(("req", "ad")),
        P(),
        P(),
        P(),
        P("ad", None, None),
        P("ad", None, None, None),
        P("ad", None, None),
        P("ad", None, None),
        P(),
        P(None, ("req", "ad")),
    )
    out_specs = (P(("req", "ad"), None, None), P(None, ("req", "ad")))
    return jax.shard_map(local, mesh=mesh, in_specs=in_specs, out_specs=out_specs, check_vma=False)
```

```python
import functools

import jax
import jax.numpy as jnp
from jax import lax
from jax.experimental import pallas as pl
from jax.experimental.pallas import tpu as pltpu
from jax.sharding import PartitionSpec as P

epsilon = 1e-05
CHUNKS = 2
DEPTH = 4
MESH = pl.DeviceIdType.MESH
VMEM_SPEC = pl.BlockSpec(memory_space=pltpu.VMEM)
HBM_SPEC = pl.BlockSpec(memory_space=pltpu.HBM)
NT = (((1,), (1,)), ((), ()))


def layer_kernel(
    n_q, groups, per_dev, n_req,
    ids_hbm, len_hbm, x_hbm, gain_hbm, fgain_hbm, wgu_hbm, wd_hbm, ina_hbm, outb_hbm,
    downa_hbm, downb_hbm, wh_hbm,
    back, lt_ref, lse_ref,
    ids, lens, xs, stage, mstage, recv, mrecv, normed, low_g, low_u, hidden, mixed, y,
    tmp, info, ends, end_normed, end_hidden, gain_ref, fgain_ref,
    wgu, wd, ina, outb, downa, downb, wh,
    gathered, stats, own_stats,
    isem, wsem, lsem, rsend, rrecv, msend, mrec, ysend, yrecv,
    asend, arecv, bsend, brecv, csend, crecv, ssend, srecv,
):
    f32 = jnp.float32
    bf16 = jnp.bfloat16
    q = lax.axis_index("req")
    a = lax.axis_index("ad")
    n = n_q * groups
    me = q * groups + a
    seq, width = xs.shape[1:]
    rank = downa.shape[0] // per_dev
    units = wd.shape[0]
    total_req = n * n_req
    per = groups // CHUNKS
    quarter = groups // 4
    own = 3 * quarter
    bits = groups.bit_length() - 1
    pieces_of = width // 128
    tile_f = 1024
    barrier = pltpu.get_barrier_semaphore()

    def target(k):
        t = lax.rem(me + k, n)
        return (lax.div(t, groups), lax.rem(t, groups))

    def each(low_k, high_k, action):
        def body(k, carry):
            action(k)
            return carry
        lax.fori_loop(low_k, high_k, body, 0)

    def partner(p):
        k = lax.rem(p + quarter, groups)
        t = 0
        for b in range(bits):
            u = lax.rem(lax.div(a, 1 << b), 2)
            v = lax.rem(lax.div(k, 1 << b), 2)
            t = t + (u + v - 2 * u * v) * (1 << b)
        return t

    firsts = [
        pltpu.make_async_copy(ids_hbm, ids, isem.at[0]),
        pltpu.make_async_copy(len_hbm, lens, isem.at[1]),
        pltpu.make_async_copy(x_hbm, xs, isem.at[2]),
        pltpu.make_async_copy(gain_hbm, gain_ref, isem.at[3]),
    ]
    for copy in firsts:
        copy.start()

    each(1, n, lambda k: pl.semaphore_signal(
        barrier, inc=1, device_id=target(k), device_id_type=MESH))

    loads = [
        pltpu.make_async_copy(ina_hbm, ina, wsem.at[0]),
        pltpu.make_async_copy(outb_hbm, outb, wsem.at[1]),
        pltpu.make_async_copy(fgain_hbm, fgain_ref, isem.at[4]),
    ]
    tiles = []
    for t in range(units // tile_f):
        cols = pl.ds(t * tile_f, tile_f)
        tiles.append([
            pltpu.make_async_copy(
                wgu_hbm.at[j, :, cols], wgu.at[j, :, cols], wsem.at[2 + 2 * t + j]
            )
            for j in range(2)
        ])
    at = 2 + 2 * (units // tile_f)
    downs = [
        pltpu.make_async_copy(downa_hbm, downa, wsem.at[at]),
        pltpu.make_async_copy(downb_hbm, downb, wsem.at[at + 1]),
        pltpu.make_async_copy(wd_hbm, wd, wsem.at[at + 2]),
    ]
    head_load = pltpu.make_async_copy(wh_hbm, wh, wsem.at[at + 3])
    for copy in loads + [c for pair in tiles for c in pair] + downs + [head_load]:
        copy.start()
    for copy in firsts:
        copy.wait()

    seq_at = lax.broadcasted_iota(jnp.int32, (seq, width), 0)
    tmp[...] = jnp.zeros_like(tmp)

    def fill(p):
        h = partner(p)
        pick = jnp.int32(-1)
        code = jnp.int32(0)
        size = jnp.int32(0)
        for r in range(n_req):
            i = ids[r]
            hit = lax.div(i, per_dev) == h
            pick = jnp.where(hit, r, pick)
            code = jnp.where(hit, lax.rem(i, per_dev), code)
            size = jnp.where(hit, lens[r], size)
        slot = xs[jnp.maximum(pick, 0)]
        stage[p] = slot
        end = jnp.sum(
            jnp.where(seq_at == size - 1, slot.astype(f32), 0.0), axis=0, keepdims=True
        )
        for c in range(pieces_of):
            tmp[c : c + 1, :] = end[:, c * 128 : (c + 1) * 128]
        for c, value in enumerate((code, size, pick)):
            tmp[pieces_of + c : pieces_of + c + 1, :] = jnp.full((1, 128), value).astype(f32)
        mstage[p] = tmp[...].astype(bf16)

    each(0, groups, fill)
    pl.semaphore_wait(barrier, n - 1)

    def row_copy(p):
        return pltpu.make_async_remote_copy(
            src_ref=stage.at[p], dst_ref=recv.at[p],
            send_sem=rsend.at[p], recv_sem=rrecv.at[p],
            device_id=(q, partner(p)), device_id_type=MESH,
        )

    def meta_copy(p):
        return pltpu.make_async_remote_copy(
            src_ref=mstage.at[p], dst_ref=mrecv.at[p],
            send_sem=msend.at[p], recv_sem=mrec.at[p],
            device_id=(q, partner(p)), device_id_type=MESH,
        )

    def back_copy(p):
        return pltpu.make_async_remote_copy(
            src_ref=y.at[p], dst_ref=back.at[a],
            send_sem=ysend.at[p], recv_sem=yrecv.at[p],
            device_id=(q, partner(p)), device_id_type=MESH,
        )

    own_back = pltpu.make_async_copy(y.at[own], back.at[a], lsem)

    def send_rows(p):
        row_copy(p).start()

    def take_rows(p):
        row_copy(p).wait_recv()

    spread = groups // DEPTH
    pairs = n_q // 2
    plane = pairs * spread
    core = lax.rem(q, 2)
    z = lax.div(a, spread)
    x = lax.rem(a, spread)
    column = q * spread + x
    place_me = lax.div(q, 2) * spread + x

    def deep_copy(j):
        return pltpu.make_async_remote_copy(
            src_ref=gathered.at[column, z], dst_ref=gathered.at[column, z],
            send_sem=asend.at[j], recv_sem=arecv.at[j],
            device_id=(q, lax.rem(z + j, DEPTH) * spread + x), device_id_type=MESH,
        )

    def plane_copy(m):
        t = lax.rem(place_me + m, plane)
        return pltpu.make_async_remote_copy(
            src_ref=gathered.at[column], dst_ref=gathered.at[column],
            send_sem=bsend.at[m], recv_sem=brecv.at[m],
            device_id=(2 * lax.div(t, spread) + core, z * spread + lax.rem(t, spread)),
            device_id_type=MESH,
        )

    def pass_on(m):
        t = lax.rem(place_me + plane - m, plane)
        origin = (2 * lax.div(t, spread) + core) * spread + lax.rem(t, spread)
        return pltpu.make_async_remote_copy(
            src_ref=gathered.at[origin], dst_ref=gathered.at[origin],
            send_sem=csend.at[m], recv_sem=crecv.at[m],
            device_id=(q + 1 - 2 * core, a), device_id_type=MESH,
        )

    def start_deep():
        each(1, DEPTH, lambda j: deep_copy(j).start())

    def start_plane():
        each(1, DEPTH, lambda j: deep_copy(j).wait_recv())
        each(1, plane, lambda m: plane_copy(m).start())
        pass_on(0).start()

    def start_pass():
        def relay(m):
            plane_copy(m).wait_recv()
            pass_on(m).start()
        each(1, plane, relay)

    def stat_copy(k):
        return pltpu.make_async_remote_copy(
            src_ref=own_stats, dst_ref=stats.at[me],
            send_sem=ssend.at[k], recv_sem=srecv.at[k],
            device_id=target(k), device_id_type=MESH,
        )

    gain = gain_ref[...].reshape(1, width)
    lane = lax.broadcasted_iota(jnp.int32, (1, per_dev * 2 * rank), 1)
    lane_d = lax.broadcasted_iota(jnp.int32, (1, per_dev * rank), 1)
    group_of = lax.div(lane, 2 * rank).astype(f32)
    group_d = lax.div(lane_d, rank).astype(f32)
    is_gate = lax.rem(lane, 2 * rank) < rank
    row_at = lax.broadcasted_iota(jnp.int32, (seq, width), 0).astype(f32)
    meta_lane = lax.broadcasted_iota(jnp.int32, (1, 128), 1)

    each(0, own, lambda p: meta_copy(p).start())
    each(own + 1, groups, lambda p: meta_copy(p).start())
    each(quarter, per, send_rows)
    each(0, quarter, send_rows)
    mrecv[own] = mstage[own]
    recv[own] = stage[own]

    each(0, own, lambda p: meta_copy(p).wait_recv())
    each(own + 1, groups, lambda p: meta_copy(p).wait_recv())
    for s in range(groups):
        block = mrecv[s].astype(f32)
        for c in range(pieces_of):
            ends[s : s + 1, c * 128 : (c + 1) * 128] = block[c : c + 1, :]
        for c in range(3):
            info[c, s : s + 1, :] = block[pieces_of + c : pieces_of + c + 1, :]
    end_rows = ends[...]
    mean_sq = jnp.mean(end_rows * end_rows, axis=-1, keepdims=True)
    end_normed[...] = (end_rows * lax.rsqrt(mean_sq + epsilon) * gain).astype(bf16)
    for copy in loads:
        copy.wait()
    low = lax.dot_general(end_normed[...], ina[...], NT, preferred_element_type=f32)
    here = group_of == info[0, :, : lane.shape[1]]
    end_g = jnp.where(here & is_gate, low, 0.0).astype(bf16)
    end_u = jnp.where(here & jnp.logical_not(is_gate), low, 0.0).astype(bf16)
    for t in range(units // tile_f):
        cols = pl.ds(t * tile_f, tile_f)
        for copy in tiles[t]:
            copy.wait()
        gate = jnp.dot(end_normed[...], wgu[0, :, cols], preferred_element_type=f32)
        gate = gate + jnp.dot(end_g, outb[:, cols], preferred_element_type=f32)
        up = jnp.dot(end_normed[...], wgu[1, :, cols], preferred_element_type=f32)
        up = up + jnp.dot(end_u, outb[:, cols], preferred_element_type=f32)
        end_hidden[:, cols] = (gate / (1.0 + jnp.exp(-gate)) * up).astype(bf16)
    for copy in downs:
        copy.wait()
    low_d = lax.dot_general(end_hidden[...], downa[...], NT, preferred_element_type=f32)
    low_d = jnp.where(group_d == info[0, :, : lane_d.shape[1]], low_d, 0.0).astype(bf16)
    total = ends[...] + jnp.dot(end_hidden[...], wd[...], preferred_element_type=f32) + jnp.dot(
        low_d, downb[...], preferred_element_type=f32
    )
    rows = jnp.where(info[1, :, 0:1] > 0.0, total, 0.0).astype(bf16).astype(f32)
    mean_sq = jnp.mean(rows * rows, axis=-1, keepdims=True)
    final = rows * lax.rsqrt(mean_sq + epsilon) * fgain_ref[...].reshape(1, width)
    for s in range(groups):
        info[3, s : s + 1, :] = jnp.where(
            meta_lane == 0, (q * groups + partner(s)).astype(f32), info[2, s : s + 1, :]
        )
    gathered[column, z, :, :width] = final.astype(bf16)
    gathered[column, z, :, width:] = info[3].astype(bf16)
    start_deep()

    for chunk in range(CHUNKS):
        mine = range(chunk * per, (chunk + 1) * per)
        if chunk == 0:
            each(0, per, take_rows)
            each(quarter, per, lambda p: row_copy(p).wait_send())
            each(per, own, send_rows)
            each(own + 1, groups, send_rows)
        else:
            each(per, own, take_rows)
            each(own + 1, groups, take_rows)
        for s in mine:
            v = recv[s].astype(f32)
            mean_sq = jnp.mean(v * v, axis=-1, keepdims=True)
            at = (s - chunk * per) * seq
            normed[at : at + seq, :] = (v * lax.rsqrt(mean_sq + epsilon) * gain).astype(bf16)
        low = lax.dot_general(normed[...], ina[...], NT, preferred_element_type=f32)
        for s in mine:
            at = (s - chunk * per) * seq
            here = group_of == info[0, s : s + 1, : lane.shape[1]]
            piece = low[at : at + seq]
            low_g[at : at + seq, :] = jnp.where(here & is_gate, piece, 0.0).astype(bf16)
            low_u[at : at + seq, :] = jnp.where(
                here & jnp.logical_not(is_gate), piece, 0.0
            ).astype(bf16)

        def units_step(j):
            cols = pl.ds(pl.multiple_of(j * tile_f, tile_f), tile_f)
            gate = jnp.dot(normed[...], wgu[0, :, cols], preferred_element_type=f32)
            gate = gate + jnp.dot(low_g[...], outb[:, cols], preferred_element_type=f32)
            up = jnp.dot(normed[...], wgu[1, :, cols], preferred_element_type=f32)
            up = up + jnp.dot(low_u[...], outb[:, cols], preferred_element_type=f32)
            hidden[:, cols] = (gate / (1.0 + jnp.exp(-gate)) * up).astype(bf16)

        each(0, units // tile_f, units_step)
        if chunk == 1:
            start_pass()
        low_d = lax.dot_general(hidden[...], downa[...], NT, preferred_element_type=f32)
        pieces = []
        for s in mine:
            at = (s - chunk * per) * seq
            here = group_d == info[0, s : s + 1, : lane_d.shape[1]]
            pieces.append(jnp.where(here, low_d[at : at + seq], 0.0))
        low_d = jnp.concatenate(pieces, axis=0).astype(bf16)
        mixed[...] = jnp.dot(hidden[...], wd[...], preferred_element_type=f32) + jnp.dot(
            low_d, downb[...], preferred_element_type=f32
        )
        for s in mine:
            at = (s - chunk * per) * seq
            total = recv[s].astype(f32) + mixed[at : at + seq, :]
            y[s] = jnp.where(row_at < info[1, s : s + 1, 0:1], total, 0.0).astype(bf16)
        if chunk == 0:
            each(quarter, per, lambda p: back_copy(p).start())
            each(0, quarter, lambda p: back_copy(p).start())
            start_plane()
        else:
            each(per, own, lambda p: back_copy(p).start())
            each(own + 1, groups, lambda p: back_copy(p).start())
            own_back.start()

    want = lax.broadcasted_iota(jnp.int32, (total_req, n * groups), 0)
    each(0, plane, lambda m: pass_on(m).wait_recv())
    wide = gathered[...].astype(f32).reshape(n * groups, width + 128)
    named = jnp.transpose(wide[:, width:])
    device = named[0:1, :].astype(jnp.int32)
    pick = named[1:2, :].astype(jnp.int32)
    row_id = jnp.where(pick >= 0, device * n_req + pick, -1)
    place = jnp.where(want == row_id, 1.0, 0.0).astype(bf16)
    ordered = jnp.dot(place, wide[:, :width].astype(bf16), preferred_element_type=f32)
    head_load.wait()
    logits = lax.dot_general(wh[...], ordered.astype(bf16), NT, preferred_element_type=f32)
    lt_ref[...] = logits
    top = jnp.max(logits, axis=0, keepdims=True)
    own_stats[0:1, :] = top
    own_stats[1:2, :] = jnp.sum(jnp.exp(logits - top), axis=0, keepdims=True)
    each(1, n, lambda k: stat_copy(k).start())
    stats[me] = own_stats[...]

    def settle(p):
        row_copy(p).wait_send()
        meta_copy(p).wait_send()
        back_copy(p).wait()

    each(0, quarter, settle)

    def settle_far(p):
        meta_copy(p).wait_send()
        back_copy(p).wait()

    each(quarter, per, settle_far)
    each(per, own, settle)
    each(own + 1, groups, settle)
    own_back.wait()
    each(1, DEPTH, lambda j: deep_copy(j).wait_send())
    each(1, plane, lambda m: plane_copy(m).wait_send())
    each(0, plane, lambda m: pass_on(m).wait_send())
    each(1, n, lambda k: stat_copy(k).wait())
    tops = stats[:, 0, :]
    best = jnp.max(tops, axis=0, keepdims=True)
    total = jnp.sum(stats[:, 1, :] * jnp.exp(tops - best), axis=0, keepdims=True)
    lse_ref[...] = best + jnp.log(total)


def finish_kernel(per_dev, ids_hbm, back, lt, lse, out_hbm, lp_hbm, ids, lp, sem, rsem, lsem):
    copy = pltpu.make_async_copy(ids_hbm, ids, sem)
    copy.start()
    shard = lt.shape[0]
    block = pl.cdiv(pl.cdiv(shard, lsem.shape[0]), 8) * 8
    copies = []
    for c, at in enumerate(range(0, shard, block)):
        rows = pl.ds(at, min(block, shard - at))
        lp[rows, :] = lt[rows, :] - lse[...]
        copies.append(pltpu.make_async_copy(lp.at[rows], lp_hbm.at[rows], lsem.at[c]))
        copies[-1].start()
    copy.wait()
    for r in range(out_hbm.shape[0]):
        copies.append(
            pltpu.make_async_copy(
                back.at[lax.div(ids[r], per_dev)], out_hbm.at[r], rsem.at[r]
            )
        )
        copies[-1].start()
    for copy in copies:
        copy.wait()


def finish(per_dev, ids, back, logits_t, lse):
    n_req = ids.shape[0]
    dma = pltpu.SemaphoreType.DMA
    return pl.pallas_call(
        functools.partial(finish_kernel, per_dev),
        out_shape=(
            jax.ShapeDtypeStruct((n_req,) + back.shape[1:], back.dtype),
            jax.ShapeDtypeStruct(logits_t.shape, logits_t.dtype),
        ),
        in_specs=[HBM_SPEC] + [VMEM_SPEC] * 3,
        out_specs=(HBM_SPEC, HBM_SPEC),
        scratch_shapes=[
            pltpu.SMEM((n_req,), jnp.int32),
            pltpu.VMEM(logits_t.shape, logits_t.dtype),
            dma(()), dma((n_req,)), dma((4,)),
        ],
        compiler_params=pltpu.CompilerParams(vmem_limit_bytes=8 << 20),
    )(ids, back, logits_t, lse)


def local(
    residual,
    lengths,
    adapter_ids,
    ffn_gain,
    w_gate_up,
    w_down,
    adapter_input_first,
    ad_out_b,
    ad_down_a,
    adapter_down_second,
    final_gain,
    head_weight,
):
    n_req, seq, width = residual.shape
    groups = lax.axis_size("ad")
    n_q = lax.axis_size("req")
    n = n_q * groups
    per_dev = adapter_input_first.shape[0]
    rank = ad_down_a.shape[1]
    units = w_down.shape[0]
    shard = head_weight.shape[1]
    total_req = n * n_req
    rows = groups // CHUNKS * seq
    plane = n // (2 * DEPTH)
    f32 = jnp.float32
    bf16 = jnp.bfloat16
    ina = adapter_input_first.reshape(per_dev * 2 * rank, width)
    outb = ad_out_b.reshape(per_dev * 2 * rank, units)
    downa = ad_down_a.reshape(per_dev * rank, units)
    downb = adapter_down_second.reshape(per_dev * rank, width)
    head_t = head_weight.T
    dma = pltpu.SemaphoreType.DMA
    vm = pltpu.VMEM
    back, logits_t, lse = pl.pallas_call(
        functools.partial(layer_kernel, n_q, groups, per_dev, n_req),
        out_shape=(
            vm((groups, seq, width), bf16),
            vm((shard, total_req), f32),
            vm((1, total_req), f32),
        ),
        in_specs=[HBM_SPEC] * 12,
        out_specs=(VMEM_SPEC,) * 3,
        scratch_shapes=[
            pltpu.SMEM((n_req,), jnp.int32),
            pltpu.SMEM((n_req,), jnp.int32),
            vm((n_req, seq, width), bf16),
            vm((groups, seq, width), bf16),
            vm((groups, 16, 128), bf16),
            vm((groups, seq, width), bf16),
            vm((groups, 16, 128), bf16),
            vm((rows, width), bf16),
            vm((rows, per_dev * 2 * rank), bf16),
            vm((rows, per_dev * 2 * rank), bf16),
            vm((rows, units), bf16),
            vm((rows, width), f32),
            vm((groups, seq, width), bf16),
            vm((16, 128), f32),
            vm((4, groups, 128), f32),
            vm((groups, width), f32),
            vm((groups, width), bf16),
            vm((groups, units), bf16),
            vm(ffn_gain.shape, f32),
            vm(final_gain.shape, f32),
            vm(w_gate_up.shape, bf16),
            vm(w_down.shape, bf16),
            vm(ina.shape, bf16),
            vm(outb.shape, bf16),
            vm(downa.shape, bf16),
            vm(downb.shape, bf16),
            vm(head_t.shape, bf16),
            vm((n // DEPTH, DEPTH, groups, width + 128), bf16),
            vm((n, 2, total_req), f32),
            vm((2, total_req), f32),
            dma((5,)), dma((12,)), dma(()),
            dma((groups,)), dma((groups,)), dma((groups,)), dma((groups,)),
            dma((groups,)), dma((groups,)),
            dma((DEPTH,)), dma((DEPTH,)),
            dma((plane,)), dma((plane,)), dma((plane,)), dma((plane,)),
            dma((n,)), dma((n,)),
        ],
        compiler_params=pltpu.CompilerParams(
            collective_id=0, has_side_effects=True, vmem_limit_bytes=52 << 20
        ),
    )(*[
        pltpu.with_memory_space_constraint(v, pltpu.HBM)
        for v in (
            adapter_ids, lengths, residual, ffn_gain, final_gain, w_gate_up, w_down,
            ina, outb, downa, downb, head_t,
        )
    ])
    layer_out, log_probs = finish(per_dev, adapter_ids, back, logits_t, lse)
    return layer_out, log_probs.T


def solution(mesh):
    in_specs = (
        P(("req", "ad"), None, None),
        P(("req", "ad")),
        P(("req", "ad")),
        P(),
        P(),
        P(),
        P("ad", None, None),
        P("ad", None, None, None),
        P("ad", None, None),
        P("ad", None, None),
        P(),
        P(None, ("req", "ad")),
    )
    out_specs = (P(("req", "ad"), None, None), P(None, ("req", "ad")))
    return jax.shard_map(local, mesh=mesh, in_specs=in_specs, out_specs=out_specs, check_vma=False)
```

```python
import functools

import jax
import jax.numpy as jnp
from jax import lax
from jax.experimental import pallas as pl
from jax.experimental.pallas import tpu as pltpu
from jax.sharding import PartitionSpec as P

epsilon = 1e-05
CHUNKS = 2
DEPTH = 4
MESH = pl.DeviceIdType.MESH
VMEM_SPEC = pl.BlockSpec(memory_space=pltpu.VMEM)
HBM_SPEC = pl.BlockSpec(memory_space=pltpu.HBM)
NT = (((1,), (1,)), ((), ()))


def layer_kernel(
    n_q, groups, per_dev, n_req,
    ids_hbm, len_hbm, x_hbm, gain_hbm, fgain_hbm, wgu_hbm, wd_hbm, ina_hbm, outb_hbm,
    downa_hbm, downb_hbm, wh_hbm,
    back, lt_ref, lse_ref,
    ids, lens, xs, stage, mstage, recv, mrecv, normed, low_g, low_u, hidden, mixed, y,
    tmp, info, ends, end_normed, end_hidden, low_ends, gain_ref, fgain_ref,
    wgu, wd, ina, outb, downa, downb, wh,
    gathered, kept, stats, own_stats,
    isem, wsem, lsem, rsend, rrecv, msend, mrec, ysend, yrecv,
    asend, arecv, bsend, brecv, csend, crecv, ssend, srecv,
):
    f32 = jnp.float32
    bf16 = jnp.bfloat16
    q = lax.axis_index("req")
    a = lax.axis_index("ad")
    n = n_q * groups
    me = q * groups + a
    seq, width = xs.shape[1:]
    rank = downa.shape[0] // per_dev
    units = wd.shape[0]
    total_req = n * n_req
    slots = n * groups
    per = groups // CHUNKS
    shift = 3 * groups // 8
    near = groups // 2 - shift
    own = groups - shift
    bits = groups.bit_length() - 1
    pieces_of = width // 128
    tile_f = 1024
    barrier = pltpu.get_barrier_semaphore()

    def target(k):
        t = lax.rem(me + k, n)
        return (lax.div(t, groups), lax.rem(t, groups))

    def each(low_k, high_k, action):
        def body(k, carry):
            action(k)
            return carry
        lax.fori_loop(low_k, high_k, body, 0)

    def partner(p):
        k = lax.rem(p + shift, groups)
        t = 0
        for b in range(bits):
            u = lax.rem(lax.div(a, 1 << b), 2)
            v = lax.rem(lax.div(k, 1 << b), 2)
            t = t + (u + v - 2 * u * v) * (1 << b)
        return t

    firsts = [
        pltpu.make_async_copy(ids_hbm, ids, isem.at[0]),
        pltpu.make_async_copy(len_hbm, lens, isem.at[1]),
        pltpu.make_async_copy(x_hbm, xs, isem.at[2]),
        pltpu.make_async_copy(gain_hbm, gain_ref, isem.at[3]),
    ]
    for copy in firsts:
        copy.start()

    each(1, n, lambda k: pl.semaphore_signal(
        barrier, inc=1, device_id=target(k), device_id_type=MESH))

    loads = [
        pltpu.make_async_copy(ina_hbm, ina, wsem.at[0]),
        pltpu.make_async_copy(outb_hbm, outb, wsem.at[1]),
        pltpu.make_async_copy(fgain_hbm, fgain_ref, isem.at[4]),
    ]
    tiles = []
    for t in range(units // tile_f):
        cols = pl.ds(t * tile_f, tile_f)
        tiles.append([
            pltpu.make_async_copy(
                wgu_hbm.at[j, :, cols], wgu.at[j, :, cols], wsem.at[2 + 2 * t + j]
            )
            for j in range(2)
        ])
    at = 2 + 2 * (units // tile_f)
    downs = [
        pltpu.make_async_copy(downa_hbm, downa, wsem.at[at]),
        pltpu.make_async_copy(downb_hbm, downb, wsem.at[at + 1]),
        pltpu.make_async_copy(wd_hbm, wd, wsem.at[at + 2]),
    ]
    head_load = pltpu.make_async_copy(wh_hbm, wh, wsem.at[at + 3])
    for copy in loads + [c for pair in tiles for c in pair] + downs + [head_load]:
        copy.start()
    for copy in firsts:
        copy.wait()

    seq_at = lax.broadcasted_iota(jnp.int32, (seq, width), 0)
    tmp[...] = jnp.zeros_like(tmp)

    def fill(p):
        h = partner(p)
        pick = jnp.int32(-1)
        code = jnp.int32(0)
        size = jnp.int32(0)
        for r in range(n_req):
            i = ids[r]
            hit = lax.div(i, per_dev) == h
            pick = jnp.where(hit, r, pick)
            code = jnp.where(hit, lax.rem(i, per_dev), code)
            size = jnp.where(hit, lens[r], size)
        slot = xs[jnp.maximum(pick, 0)]
        stage[p] = slot
        end = jnp.sum(
            jnp.where(seq_at == size - 1, slot.astype(f32), 0.0), axis=0, keepdims=True
        )
        for c in range(pieces_of):
            tmp[c : c + 1, :] = end[:, c * 128 : (c + 1) * 128]
        for c, value in enumerate((code, size, pick)):
            tmp[pieces_of + c : pieces_of + c + 1, :] = jnp.full((1, 128), value).astype(f32)
        mstage[p] = tmp[...].astype(bf16)

    each(0, groups, fill)
    pl.semaphore_wait(barrier, n - 1)

    def row_copy(p):
        return pltpu.make_async_remote_copy(
            src_ref=stage.at[p], dst_ref=recv.at[p],
            send_sem=rsend.at[p], recv_sem=rrecv.at[p],
            device_id=(q, partner(p)), device_id_type=MESH,
        )

    def meta_copy(p):
        return pltpu.make_async_remote_copy(
            src_ref=mstage.at[p], dst_ref=mrecv.at[p],
            send_sem=msend.at[p], recv_sem=mrec.at[p],
            device_id=(q, partner(p)), device_id_type=MESH,
        )

    def back_copy(p):
        return pltpu.make_async_remote_copy(
            src_ref=y.at[p], dst_ref=back.at[a],
            send_sem=ysend.at[p], recv_sem=yrecv.at[p],
            device_id=(q, partner(p)), device_id_type=MESH,
        )

    own_back = pltpu.make_async_copy(y.at[own], back.at[a], lsem)

    def send_rows(p):
        row_copy(p).start()

    def take_rows(p):
        row_copy(p).wait_recv()

    spread = groups // DEPTH
    pairs = n_q // 2
    plane = pairs * spread
    core = lax.rem(q, 2)
    z = lax.div(a, spread)
    x = lax.rem(a, spread)
    column = q * spread + x
    place_me = lax.div(q, 2) * spread + x

    def level(j):
        t = 0
        for b in range(DEPTH.bit_length() - 1):
            u = lax.rem(lax.div(z, 1 << b), 2)
            v = lax.rem(lax.div(j, 1 << b), 2)
            t = t + (u + v - 2 * u * v) * (1 << b)
        return t

    def deep_copy(j):
        return pltpu.make_async_remote_copy(
            src_ref=gathered.at[column, z], dst_ref=gathered.at[column, z],
            send_sem=asend.at[j], recv_sem=arecv.at[j],
            device_id=(q, level(j) * spread + x), device_id_type=MESH,
        )

    def plane_copy(j, m):
        t = lax.rem(place_me + m, plane)
        return pltpu.make_async_remote_copy(
            src_ref=gathered.at[column, level(j)], dst_ref=gathered.at[column, level(j)],
            send_sem=bsend.at[j, m], recv_sem=brecv.at[j, m],
            device_id=(2 * lax.div(t, spread) + core, z * spread + lax.rem(t, spread)),
            device_id_type=MESH,
        )

    def pass_on(m):
        t = lax.rem(place_me + plane - m, plane)
        origin = (2 * lax.div(t, spread) + core) * spread + lax.rem(t, spread)
        return pltpu.make_async_remote_copy(
            src_ref=gathered.at[origin], dst_ref=gathered.at[origin],
            send_sem=csend.at[m], recv_sem=crecv.at[m],
            device_id=(q + 1 - 2 * core, a), device_id_type=MESH,
        )

    def start_deep():
        each(1, DEPTH, lambda j: deep_copy(j).start())
        each(1, plane, lambda m: plane_copy(jnp.int32(0), m).start())

    def forward(j):
        deep_copy(j).wait_recv()
        each(1, plane, lambda m: plane_copy(j, m).start())

    def start_pass():
        pass_on(0).start()

        def relay(m):
            each(0, DEPTH, lambda j: plane_copy(j, m).wait_recv())
            pass_on(m).start()

        each(1, plane, relay)

    def stat_copy(k):
        return pltpu.make_async_remote_copy(
            src_ref=own_stats, dst_ref=stats.at[me],
            send_sem=ssend.at[k], recv_sem=srecv.at[k],
            device_id=target(k), device_id_type=MESH,
        )

    gain = gain_ref[...].reshape(1, width)
    lane = lax.broadcasted_iota(jnp.int32, (1, per_dev * 2 * rank), 1)
    lane_d = lax.broadcasted_iota(jnp.int32, (1, per_dev * rank), 1)
    group_of = lax.div(lane, 2 * rank).astype(f32)
    group_d = lax.div(lane_d, rank).astype(f32)
    is_gate = lax.rem(lane, 2 * rank) < rank
    row_at = lax.broadcasted_iota(jnp.int32, (seq, width), 0).astype(f32)
    meta_lane = lax.broadcasted_iota(jnp.int32, (1, 128), 1)

    each(0, own, lambda p: meta_copy(p).start())
    each(own + 1, groups, lambda p: meta_copy(p).start())
    each(near, per, send_rows)
    each(0, near, send_rows)
    mrecv[own] = mstage[own]
    recv[own] = stage[own]

    each(0, own, lambda p: meta_copy(p).wait_recv())
    each(own + 1, groups, lambda p: meta_copy(p).wait_recv())
    for s in range(groups):
        block = mrecv[s].astype(f32)
        for c in range(pieces_of):
            ends[s : s + 1, c * 128 : (c + 1) * 128] = block[c : c + 1, :]
        for c in range(3):
            info[c, s : s + 1, :] = block[pieces_of + c : pieces_of + c + 1, :]
    end_rows = ends[...]
    mean_sq = jnp.mean(end_rows * end_rows, axis=-1, keepdims=True)
    end_normed[...] = (end_rows * lax.rsqrt(mean_sq + epsilon) * gain).astype(bf16)
    for copy in loads:
        copy.wait()
    low = lax.dot_general(end_normed[...], ina[...], NT, preferred_element_type=f32)
    here = group_of == info[0, :, : lane.shape[1]]
    end_g = jnp.where(here & is_gate, low, 0.0).astype(bf16)
    end_u = jnp.where(here & jnp.logical_not(is_gate), low, 0.0).astype(bf16)
    low_ends[0] = end_g
    low_ends[1] = end_u

    def end_step(t):
        cols = pl.ds(pl.multiple_of(t * tile_f, tile_f), tile_f)
        for i in range(2):
            pltpu.make_async_copy(
                wgu_hbm.at[i, :, cols], wgu.at[i, :, cols], wsem.at[2 + 2 * t + i]
            ).wait()
        gate = jnp.dot(end_normed[...], wgu[0, :, cols], preferred_element_type=f32)
        gate = gate + jnp.dot(low_ends[0], outb[:, cols], preferred_element_type=f32)
        up = jnp.dot(end_normed[...], wgu[1, :, cols], preferred_element_type=f32)
        up = up + jnp.dot(low_ends[1], outb[:, cols], preferred_element_type=f32)
        end_hidden[:, cols] = (gate / (1.0 + jnp.exp(-gate)) * up).astype(bf16)

    each(0, units // tile_f, end_step)
    for copy in downs:
        copy.wait()
    low_d = lax.dot_general(end_hidden[...], downa[...], NT, preferred_element_type=f32)
    low_d = jnp.where(group_d == info[0, :, : lane_d.shape[1]], low_d, 0.0).astype(bf16)
    total = ends[...] + jnp.dot(end_hidden[...], wd[...], preferred_element_type=f32) + jnp.dot(
        low_d, downb[...], preferred_element_type=f32
    )
    rows = jnp.where(info[1, :, 0:1] > 0.0, total, 0.0).astype(bf16).astype(f32)
    mean_sq = jnp.mean(rows * rows, axis=-1, keepdims=True)
    final = rows * lax.rsqrt(mean_sq + epsilon) * fgain_ref[...].reshape(1, width)
    for s in range(groups):
        info[3, s : s + 1, :] = jnp.where(
            meta_lane == 0, (q * groups + partner(s)).astype(f32), info[2, s : s + 1, :]
        )
    gathered[column, z, :, :width] = final.astype(bf16)
    gathered[column, z, :, width:] = info[3].astype(bf16)
    start_deep()

    def units_step(j):
        cols = pl.ds(pl.multiple_of(j * tile_f, tile_f), tile_f)
        gate = jnp.dot(normed[...], wgu[0, :, cols], preferred_element_type=f32)
        gate = gate + jnp.dot(low_g[...], outb[:, cols], preferred_element_type=f32)
        up = jnp.dot(normed[...], wgu[1, :, cols], preferred_element_type=f32)
        up = up + jnp.dot(low_u[...], outb[:, cols], preferred_element_type=f32)
        hidden[:, cols] = (gate / (1.0 + jnp.exp(-gate)) * up).astype(bf16)

    def head_part():
        each(0, plane, lambda m: pass_on(m).wait_recv())
        wide = gathered[...].astype(f32).reshape(slots, width + 128)
        kept[...] = wide[:, :width].astype(bf16)
        head_load.wait()
        loose = lax.dot_general(wh[...], kept[...], NT, preferred_element_type=f32)
        top = jnp.max(loose, axis=0, keepdims=True)
        own_stats[0:1, :] = top
        own_stats[1:2, :] = jnp.sum(jnp.exp(loose - top), axis=0, keepdims=True)
        each(1, n, lambda k: stat_copy(k).start())
        stats[me] = own_stats[...]

    def chunk_step(chunk):
        first = chunk * per

        @pl.when(chunk == 0)
        def _():
            each(0, per, take_rows)
            each(near, per, lambda p: row_copy(p).wait_send())
            each(per, own, send_rows)
            each(own + 1, groups, send_rows)

        @pl.when(chunk == 1)
        def _():
            each(per, own, take_rows)
            each(own + 1, groups, take_rows)

        for i in range(per):
            v = recv[first + i].astype(f32)
            mean_sq = jnp.mean(v * v, axis=-1, keepdims=True)
            normed[i * seq : (i + 1) * seq, :] = (
                v * lax.rsqrt(mean_sq + epsilon) * gain
            ).astype(bf16)
        @pl.when(chunk == 1)
        def _():
            start_pass()

        low = lax.dot_general(normed[...], ina[...], NT, preferred_element_type=f32)
        notes = [mrecv[first + i].astype(f32) for i in range(per)]
        for i in range(per):
            at = i * seq
            here = group_of == notes[i][pieces_of : pieces_of + 1, : lane.shape[1]]
            piece = low[at : at + seq]
            low_g[at : at + seq, :] = jnp.where(here & is_gate, piece, 0.0).astype(bf16)
            low_u[at : at + seq, :] = jnp.where(
                here & jnp.logical_not(is_gate), piece, 0.0
            ).astype(bf16)
        def units_forward(j):
            units_step(j)

            @pl.when((chunk == 0) & (j < DEPTH - 1))
            def _():
                forward(j + 1)

        each(0, units // tile_f, units_forward)

        @pl.when(chunk == 0)
        def _():
            each(units // tile_f + 1, DEPTH, forward)

        @pl.when(chunk == 1)
        def _():
            head_part()

        low_d = lax.dot_general(hidden[...], downa[...], NT, preferred_element_type=f32)
        pieces = []
        for i in range(per):
            here = group_d == notes[i][pieces_of : pieces_of + 1, : lane_d.shape[1]]
            pieces.append(jnp.where(here, low_d[i * seq : (i + 1) * seq], 0.0))
        low_d = jnp.concatenate(pieces, axis=0).astype(bf16)
        mixed[...] = jnp.dot(hidden[...], wd[...], preferred_element_type=f32) + jnp.dot(
            low_d, downb[...], preferred_element_type=f32
        )
        for i in range(per):
            size = notes[i][pieces_of + 1 : pieces_of + 2, 0:1]
            total = recv[first + i].astype(f32) + mixed[i * seq : (i + 1) * seq, :]
            y[first + i] = jnp.where(row_at < size, total, 0.0).astype(bf16)

        @pl.when(chunk == 0)
        def _():
            each(near, per, lambda p: back_copy(p).start())
            each(0, near, lambda p: back_copy(p).start())

        @pl.when(chunk == 1)
        def _():
            each(per, own, lambda p: back_copy(p).start())
            each(own + 1, groups, lambda p: back_copy(p).start())
            own_back.start()

    each(0, CHUNKS, chunk_step)

    want = lax.broadcasted_iota(jnp.int32, (total_req, slots), 0)

    names = gathered[:, :, :, width:].astype(f32).reshape(slots, 128)
    named = jnp.transpose(names)
    row_id = jnp.where(named[1:2, :] >= 0.0, named[0:1, :] * n_req + named[1:2, :], -1.0)
    place = jnp.where(want == row_id.astype(jnp.int32), 1.0, 0.0).astype(bf16)
    ordered = jnp.dot(place, kept[...], preferred_element_type=f32).astype(bf16)
    lt_ref[...] = lax.dot_general(wh[...], ordered, NT, preferred_element_type=f32)
    slot_id = jnp.where(names[:, 1:2] >= 0.0, names[:, 0:1] * n_req + names[:, 1:2], -1.0)

    def settle(p):
        row_copy(p).wait_send()
        meta_copy(p).wait_send()
        back_copy(p).wait()

    each(0, near, settle)

    def settle_far(p):
        meta_copy(p).wait_send()
        back_copy(p).wait()

    each(near, per, settle_far)
    each(per, own, settle)
    each(own + 1, groups, settle)
    own_back.wait()
    each(1, DEPTH, lambda j: deep_copy(j).wait_send())
    each(0, DEPTH, lambda j: each(1, plane, lambda m: plane_copy(j, m).wait_send()))
    each(0, plane, lambda m: pass_on(m).wait_send())
    each(1, n, lambda k: stat_copy(k).wait())
    tops = stats[:, 0, :]
    best = jnp.max(tops, axis=0, keepdims=True)
    total = jnp.sum(stats[:, 1, :] * jnp.exp(tops - best), axis=0, keepdims=True)
    lse = jnp.transpose(jnp.broadcast_to(best + jnp.log(total), (8, slots)))[:, 0:1]
    across = lax.broadcasted_iota(jnp.int32, (slots, total_req), 1)
    chosen = across == slot_id.astype(jnp.int32)
    lse_ref[...] = jnp.sum(jnp.where(chosen, lse, 0.0), axis=0, keepdims=True)


def finish_kernel(per_dev, ids_hbm, back, lt, lse, out_hbm, lp_hbm, ids, lp, sem, rsem, lsem):
    copy = pltpu.make_async_copy(ids_hbm, ids, sem)
    copy.start()
    shard = lt.shape[0]
    block = pl.cdiv(pl.cdiv(shard, lsem.shape[0]), 8) * 8
    copies = []
    for c, at in enumerate(range(0, shard, block)):
        rows = pl.ds(at, min(block, shard - at))
        lp[rows, :] = lt[rows, :] - lse[...]
        copies.append(pltpu.make_async_copy(lp.at[rows], lp_hbm.at[rows], lsem.at[c]))
        copies[-1].start()
    copy.wait()
    for r in range(out_hbm.shape[0]):
        copies.append(
            pltpu.make_async_copy(
                back.at[lax.div(ids[r], per_dev)], out_hbm.at[r], rsem.at[r]
            )
        )
        copies[-1].start()
    for copy in copies:
        copy.wait()


def finish(per_dev, ids, back, logits_t, lse):
    n_req = ids.shape[0]
    dma = pltpu.SemaphoreType.DMA
    return pl.pallas_call(
        functools.partial(finish_kernel, per_dev),
        out_shape=(
            jax.ShapeDtypeStruct((n_req,) + back.shape[1:], back.dtype),
            jax.ShapeDtypeStruct(logits_t.shape, logits_t.dtype),
        ),
        in_specs=[HBM_SPEC] + [VMEM_SPEC] * 3,
        out_specs=(HBM_SPEC, HBM_SPEC),
        scratch_shapes=[
            pltpu.SMEM((n_req,), jnp.int32),
            pltpu.VMEM(logits_t.shape, logits_t.dtype),
            dma(()), dma((n_req,)), dma((4,)),
        ],
        compiler_params=pltpu.CompilerParams(vmem_limit_bytes=8 << 20),
    )(ids, back, logits_t, lse)


def local(
    residual,
    lengths,
    adapter_ids,
    ffn_gain,
    w_gate_up,
    w_down,
    adapter_input_first,
    ad_out_b,
    ad_down_a,
    adapter_down_second,
    final_gain,
    head_weight,
):
    n_req, seq, width = residual.shape
    groups = lax.axis_size("ad")
    n_q = lax.axis_size("req")
    n = n_q * groups
    per_dev = adapter_input_first.shape[0]
    rank = ad_down_a.shape[1]
    units = w_down.shape[0]
    shard = head_weight.shape[1]
    total_req = n * n_req
    slots = n * groups
    rows = groups // CHUNKS * seq
    plane = n // (2 * DEPTH)
    f32 = jnp.float32
    bf16 = jnp.bfloat16
    ina = adapter_input_first.reshape(per_dev * 2 * rank, width)
    outb = ad_out_b.reshape(per_dev * 2 * rank, units)
    downa = ad_down_a.reshape(per_dev * rank, units)
    downb = adapter_down_second.reshape(per_dev * rank, width)
    head_t = head_weight.T
    dma = pltpu.SemaphoreType.DMA
    vm = pltpu.VMEM
    back, logits_t, lse = pl.pallas_call(
        functools.partial(layer_kernel, n_q, groups, per_dev, n_req),
        out_shape=(
            vm((groups, seq, width), bf16),
            vm((shard, total_req), f32),
            vm((1, total_req), f32),
        ),
        in_specs=[HBM_SPEC] * 12,
        out_specs=(VMEM_SPEC,) * 3,
        scratch_shapes=[
            pltpu.SMEM((n_req,), jnp.int32),
            pltpu.SMEM((n_req,), jnp.int32),
            vm((n_req, seq, width), bf16),
            vm((groups, seq, width), bf16),
            vm((groups, 16, 128), bf16),
            vm((groups, seq, width), bf16),
            vm((groups, 16, 128), bf16),
            vm((rows, width), bf16),
            vm((rows, per_dev * 2 * rank), bf16),
            vm((rows, per_dev * 2 * rank), bf16),
            vm((rows, units), bf16),
            vm((rows, width), f32),
            vm((groups, seq, width), bf16),
            vm((16, 128), f32),
            vm((4, groups, 128), f32),
            vm((groups, width), f32),
            vm((groups, width), bf16),
            vm((groups, units), bf16),
            vm((2, groups, per_dev * 2 * rank), bf16),
            vm(ffn_gain.shape, f32),
            vm(final_gain.shape, f32),
            vm(w_gate_up.shape, bf16),
            vm(w_down.shape, bf16),
            vm(ina.shape, bf16),
            vm(outb.shape, bf16),
            vm(downa.shape, bf16),
            vm(downb.shape, bf16),
            vm(head_t.shape, bf16),
            vm((n // DEPTH, DEPTH, groups, width + 128), bf16),
            vm((slots, width), bf16),
            vm((n, 2, slots), f32),
            vm((2, slots), f32),
            dma((5,)), dma((12,)), dma(()),
            dma((groups,)), dma((groups,)), dma((groups,)), dma((groups,)),
            dma((groups,)), dma((groups,)),
            dma((DEPTH,)), dma((DEPTH,)),
            dma((DEPTH, plane)), dma((DEPTH, plane)), dma((plane,)), dma((plane,)),
            dma((n,)), dma((n,)),
        ],
        compiler_params=pltpu.CompilerParams(
            collective_id=0, has_side_effects=True, vmem_limit_bytes=60 << 20
        ),
    )(*[
        pltpu.with_memory_space_constraint(v, pltpu.HBM)
        for v in (
            adapter_ids, lengths, residual, ffn_gain, final_gain, w_gate_up, w_down,
            ina, outb, downa, downb, head_t,
        )
    ])
    layer_out, log_probs = finish(per_dev, adapter_ids, back, logits_t, lse)
    return layer_out, log_probs.T


def solution(mesh):
    in_specs = (
        P(("req", "ad"), None, None),
        P(("req", "ad")),
        P(("req", "ad")),
        P(),
        P(),
        P(),
        P("ad", None, None),
        P("ad", None, None, None),
        P("ad", None, None),
        P("ad", None, None),
        P(),
        P(None, ("req", "ad")),
    )
    out_specs = (P(("req", "ad"), None, None), P(None, ("req", "ad")))
    return jax.shard_map(local, mesh=mesh, in_specs=in_specs, out_specs=out_specs, check_vma=False)
```

```python
import functools

import jax
import jax.numpy as jnp
from jax import lax
from jax.experimental import pallas as pl
from jax.experimental.pallas import tpu as pltpu
from jax.sharding import PartitionSpec as P

epsilon = 1e-05
CHUNKS = 2
DEPTH = 4
MESH = pl.DeviceIdType.MESH
VMEM_SPEC = pl.BlockSpec(memory_space=pltpu.VMEM)
HBM_SPEC = pl.BlockSpec(memory_space=pltpu.HBM)
NT = (((1,), (1,)), ((), ()))


def layer_kernel(
    n_q, groups, per_dev, n_req,
    ids_hbm, len_hbm, x_hbm, gain_hbm, fgain_hbm, wgu_hbm, wd_hbm, ina_hbm, outb_hbm,
    downa_hbm, downb_hbm, wh_hbm,
    back, lt_ref, lse_ref,
    ids, lens, xs, stage, mstage, recv, mrecv, normed, low_g, low_u, hidden, mixed, y,
    tmp, info, ends, end_normed, end_hidden, low_ends, gain_ref, fgain_ref,
    wgu, wd, ina, outb, downa, turned, downb, wh,
    gathered, kept, stats, own_stats,
    isem, wsem, lsem, rsend, rrecv, msend, mrec, ysend, yrecv,
    asend, arecv, bsend, brecv, csend, crecv, ssend, srecv,
):
    f32 = jnp.float32
    bf16 = jnp.bfloat16
    q = lax.axis_index("req")
    a = lax.axis_index("ad")
    n = n_q * groups
    me = q * groups + a
    seq, width = xs.shape[1:]
    rank = downa.shape[0] // per_dev
    units = wd.shape[0]
    total_req = n * n_req
    slots = n * groups
    per = groups // CHUNKS
    shift = 3 * groups // 8
    near = groups // 2 - shift
    own = groups - shift
    bits = groups.bit_length() - 1
    pieces_of = width // 128
    tile_f = 1024
    barrier = pltpu.get_barrier_semaphore()

    def target(k):
        t = lax.rem(me + k, n)
        return (lax.div(t, groups), lax.rem(t, groups))

    def each(low_k, high_k, action):
        def body(k, carry):
            action(k)
            return carry
        lax.fori_loop(low_k, high_k, body, 0)

    def partner(p):
        k = lax.rem(p + shift, groups)
        t = 0
        for b in range(bits):
            u = lax.rem(lax.div(a, 1 << b), 2)
            v = lax.rem(lax.div(k, 1 << b), 2)
            t = t + (u + v - 2 * u * v) * (1 << b)
        return t

    firsts = [
        pltpu.make_async_copy(ids_hbm, ids, isem.at[0]),
        pltpu.make_async_copy(len_hbm, lens, isem.at[1]),
        pltpu.make_async_copy(x_hbm, xs, isem.at[2]),
        pltpu.make_async_copy(gain_hbm, gain_ref, isem.at[3]),
    ]
    for copy in firsts:
        copy.start()

    each(1, n, lambda k: pl.semaphore_signal(
        barrier, inc=1, device_id=target(k), device_id_type=MESH))

    loads = [
        pltpu.make_async_copy(ina_hbm, ina, wsem.at[0]),
        pltpu.make_async_copy(outb_hbm, outb, wsem.at[1]),
        pltpu.make_async_copy(fgain_hbm, fgain_ref, isem.at[4]),
    ]
    tiles = []
    for t in range(units // tile_f):
        cols = pl.ds(t * tile_f, tile_f)
        tiles.append([
            pltpu.make_async_copy(
                wgu_hbm.at[j, :, cols], wgu.at[j, :, cols], wsem.at[2 + 2 * t + j]
            )
            for j in range(2)
        ])
    at = 2 + 2 * (units // tile_f)
    downs = [
        pltpu.make_async_copy(downa_hbm, downa, wsem.at[at]),
        pltpu.make_async_copy(downb_hbm, downb, wsem.at[at + 1]),
        pltpu.make_async_copy(wd_hbm, wd, wsem.at[at + 2]),
    ]
    head_load = pltpu.make_async_copy(wh_hbm, wh, wsem.at[at + 3])
    for copy in loads + [c for pair in tiles for c in pair] + downs + [head_load]:
        copy.start()
    for copy in firsts:
        copy.wait()

    seq_at = lax.broadcasted_iota(jnp.int32, (seq, width), 0)
    tmp[...] = jnp.zeros_like(tmp)

    def fill(p):
        h = partner(p)
        pick = jnp.int32(-1)
        code = jnp.int32(0)
        size = jnp.int32(0)
        for r in range(n_req):
            i = ids[r]
            hit = lax.div(i, per_dev) == h
            pick = jnp.where(hit, r, pick)
            code = jnp.where(hit, lax.rem(i, per_dev), code)
            size = jnp.where(hit, lens[r], size)
        slot = xs[jnp.maximum(pick, 0)]
        stage[p] = slot
        end = jnp.sum(
            jnp.where(seq_at == size - 1, slot.astype(f32), 0.0), axis=0, keepdims=True
        )
        for c in range(pieces_of):
            tmp[c : c + 1, :] = end[:, c * 128 : (c + 1) * 128]
        for c, value in enumerate((code, size, pick)):
            tmp[pieces_of + c : pieces_of + c + 1, :] = jnp.full((1, 128), value).astype(f32)
        mstage[p] = tmp[...].astype(bf16)

    each(0, groups, fill)
    pl.semaphore_wait(barrier, n - 1)

    def row_copy(p):
        return pltpu.make_async_remote_copy(
            src_ref=stage.at[p], dst_ref=recv.at[p],
            send_sem=rsend.at[p], recv_sem=rrecv.at[p],
            device_id=(q, partner(p)), device_id_type=MESH,
        )

    def meta_copy(p):
        return pltpu.make_async_remote_copy(
            src_ref=mstage.at[p], dst_ref=mrecv.at[p],
            send_sem=msend.at[p], recv_sem=mrec.at[p],
            device_id=(q, partner(p)), device_id_type=MESH,
        )

    def back_copy(p):
        return pltpu.make_async_remote_copy(
            src_ref=y.at[p], dst_ref=back.at[a],
            send_sem=ysend.at[p], recv_sem=yrecv.at[p],
            device_id=(q, partner(p)), device_id_type=MESH,
        )

    own_back = pltpu.make_async_copy(y.at[own], back.at[a], lsem)

    def send_rows(p):
        row_copy(p).start()

    def take_rows(p):
        row_copy(p).wait_recv()

    spread = groups // DEPTH
    pairs = n_q // 2
    plane = pairs * spread
    core = lax.rem(q, 2)
    z = lax.div(a, spread)
    x = lax.rem(a, spread)
    column = q * spread + x
    place_me = lax.div(q, 2) * spread + x

    def level(j):
        t = 0
        for b in range(DEPTH.bit_length() - 1):
            u = lax.rem(lax.div(z, 1 << b), 2)
            v = lax.rem(lax.div(j, 1 << b), 2)
            t = t + (u + v - 2 * u * v) * (1 << b)
        return t

    def deep_copy(j):
        return pltpu.make_async_remote_copy(
            src_ref=gathered.at[column, z], dst_ref=gathered.at[column, z],
            send_sem=asend.at[j], recv_sem=arecv.at[j],
            device_id=(q, level(j) * spread + x), device_id_type=MESH,
        )

    def plane_copy(j, m):
        t = lax.rem(place_me + m, plane)
        return pltpu.make_async_remote_copy(
            src_ref=gathered.at[column, level(j)], dst_ref=gathered.at[column, level(j)],
            send_sem=bsend.at[j, m], recv_sem=brecv.at[j, m],
            device_id=(2 * lax.div(t, spread) + core, z * spread + lax.rem(t, spread)),
            device_id_type=MESH,
        )

    def pass_on(m):
        t = lax.rem(place_me + plane - m, plane)
        origin = (2 * lax.div(t, spread) + core) * spread + lax.rem(t, spread)
        return pltpu.make_async_remote_copy(
            src_ref=gathered.at[origin], dst_ref=gathered.at[origin],
            send_sem=csend.at[m], recv_sem=crecv.at[m],
            device_id=(q + 1 - 2 * core, a), device_id_type=MESH,
        )

    def start_deep():
        each(1, DEPTH, lambda j: deep_copy(j).start())
        each(1, plane, lambda m: plane_copy(jnp.int32(0), m).start())

    def forward(j):
        deep_copy(j).wait_recv()
        each(1, plane, lambda m: plane_copy(j, m).start())

    def start_pass():
        pass_on(0).start()

        def relay(m):
            each(0, DEPTH, lambda j: plane_copy(j, m).wait_recv())
            pass_on(m).start()

        each(1, plane, relay)

    def stat_copy(k):
        return pltpu.make_async_remote_copy(
            src_ref=own_stats, dst_ref=stats.at[me],
            send_sem=ssend.at[k], recv_sem=srecv.at[k],
            device_id=target(k), device_id_type=MESH,
        )

    gain = gain_ref[...].reshape(1, width)
    lane = lax.broadcasted_iota(jnp.int32, (1, per_dev * 2 * rank), 1)
    lane_d = lax.broadcasted_iota(jnp.int32, (1, per_dev * rank), 1)
    group_of = lax.div(lane, 2 * rank).astype(f32)
    group_d = lax.div(lane_d, rank).astype(f32)
    is_gate = lax.rem(lane, 2 * rank) < rank
    row_at = lax.broadcasted_iota(jnp.int32, (seq, width), 0).astype(f32)
    meta_lane = lax.broadcasted_iota(jnp.int32, (1, 128), 1)

    each(0, own, lambda p: meta_copy(p).start())
    each(own + 1, groups, lambda p: meta_copy(p).start())
    each(near, per, send_rows)
    each(0, near, send_rows)
    mrecv[own] = mstage[own]
    recv[own] = stage[own]

    each(0, own, lambda p: meta_copy(p).wait_recv())
    each(own + 1, groups, lambda p: meta_copy(p).wait_recv())
    for s in range(groups):
        block = mrecv[s].astype(f32)
        for c in range(pieces_of):
            ends[s : s + 1, c * 128 : (c + 1) * 128] = block[c : c + 1, :]
        for c in range(3):
            info[c, s : s + 1, :] = block[pieces_of + c : pieces_of + c + 1, :]
    end_rows = ends[...]
    mean_sq = jnp.mean(end_rows * end_rows, axis=-1, keepdims=True)
    end_normed[...] = (end_rows * lax.rsqrt(mean_sq + epsilon) * gain).astype(bf16)
    for copy in loads:
        copy.wait()
    low = lax.dot_general(end_normed[...], ina[...], NT, preferred_element_type=f32)
    here = group_of == info[0, :, : lane.shape[1]]
    end_g = jnp.where(here & is_gate, low, 0.0).astype(bf16)
    end_u = jnp.where(here & jnp.logical_not(is_gate), low, 0.0).astype(bf16)
    low_ends[0] = end_g
    low_ends[1] = end_u

    def end_step(t):
        cols = pl.ds(pl.multiple_of(t * tile_f, tile_f), tile_f)
        for i in range(2):
            pltpu.make_async_copy(
                wgu_hbm.at[i, :, cols], wgu.at[i, :, cols], wsem.at[2 + 2 * t + i]
            ).wait()
        gate = jnp.dot(end_normed[...], wgu[0, :, cols], preferred_element_type=f32)
        gate = gate + jnp.dot(low_ends[0], outb[:, cols], preferred_element_type=f32)
        up = jnp.dot(end_normed[...], wgu[1, :, cols], preferred_element_type=f32)
        up = up + jnp.dot(low_ends[1], outb[:, cols], preferred_element_type=f32)
        end_hidden[:, cols] = (gate / (1.0 + jnp.exp(-gate)) * up).astype(bf16)

    each(0, units // tile_f, end_step)
    for copy in downs:
        copy.wait()
    low_d = lax.dot_general(end_hidden[...], downa[...], NT, preferred_element_type=f32)
    low_d = jnp.where(group_d == info[0, :, : lane_d.shape[1]], low_d, 0.0).astype(bf16)
    total = ends[...] + jnp.dot(end_hidden[...], wd[...], preferred_element_type=f32) + jnp.dot(
        low_d, downb[...], preferred_element_type=f32
    )
    rows = jnp.where(info[1, :, 0:1] > 0.0, total, 0.0).astype(bf16).astype(f32)
    mean_sq = jnp.mean(rows * rows, axis=-1, keepdims=True)
    final = rows * lax.rsqrt(mean_sq + epsilon) * fgain_ref[...].reshape(1, width)
    for s in range(groups):
        info[3, s : s + 1, :] = jnp.where(
            meta_lane == 0, (q * groups + partner(s)).astype(f32), info[2, s : s + 1, :]
        )
    gathered[column, z, :, :width] = final.astype(bf16)
    gathered[column, z, :, width:] = info[3].astype(bf16)
    start_deep()

    def units_step(j):
        cols = pl.ds(pl.multiple_of(j * tile_f, tile_f), tile_f)
        gate = jnp.dot(normed[...], wgu[0, :, cols], preferred_element_type=f32)
        gate = gate + jnp.dot(low_g[...], outb[:, cols], preferred_element_type=f32)
        up = jnp.dot(normed[...], wgu[1, :, cols], preferred_element_type=f32)
        up = up + jnp.dot(low_u[...], outb[:, cols], preferred_element_type=f32)
        hidden[:, cols] = (gate / (1.0 + jnp.exp(-gate)) * up).astype(bf16)

    def head_part():
        each(0, plane, lambda m: pass_on(m).wait_recv())
        wide = gathered[...].astype(f32).reshape(slots, width + 128)
        kept[...] = wide[:, :width].astype(bf16)
        head_load.wait()
        loose = lax.dot_general(wh[...], kept[...], NT, preferred_element_type=f32)
        top = jnp.max(loose, axis=0, keepdims=True)
        own_stats[0:1, :] = top
        own_stats[1:2, :] = jnp.sum(jnp.exp(loose - top), axis=0, keepdims=True)
        each(1, n, lambda k: stat_copy(k).start())
        stats[me] = own_stats[...]

    def chunk_step(chunk):
        first = chunk * per

        @pl.when(chunk == 0)
        def _():
            each(0, per, take_rows)
            each(near, per, lambda p: row_copy(p).wait_send())
            each(per, own, send_rows)
            each(own + 1, groups, send_rows)

        @pl.when(chunk == 1)
        def _():
            each(per, own, take_rows)
            each(own + 1, groups, take_rows)

        for i in range(per):
            v = recv[first + i].astype(f32)
            mean_sq = jnp.mean(v * v, axis=-1, keepdims=True)
            normed[i * seq : (i + 1) * seq, :] = (
                v * lax.rsqrt(mean_sq + epsilon) * gain
            ).astype(bf16)
        low = lax.dot_general(normed[...], ina[...], NT, preferred_element_type=f32)
        notes = [mrecv[first + i].astype(f32) for i in range(per)]
        for i in range(per):
            at = i * seq
            here = group_of == notes[i][pieces_of : pieces_of + 1, : lane.shape[1]]
            piece = low[at : at + seq]
            low_g[at : at + seq, :] = jnp.where(here & is_gate, piece, 0.0).astype(bf16)
            low_u[at : at + seq, :] = jnp.where(
                here & jnp.logical_not(is_gate), piece, 0.0
            ).astype(bf16)
        def units_forward(j):
            units_step(j)

            @pl.when((chunk == 0) & (j < DEPTH - 1))
            def _():
                forward(j + 1)

            @pl.when((chunk == 1) & (j == 0))
            def _():
                start_pass()

        each(0, units // tile_f, units_forward)

        @pl.when(chunk == 0)
        def _():
            each(units // tile_f + 1, DEPTH, forward)

        @pl.when(chunk == 1)
        def _():
            head_part()

        low_d = jnp.dot(hidden[...], turned[...], preferred_element_type=f32)
        pieces = []
        for i in range(per):
            here = group_d == notes[i][pieces_of : pieces_of + 1, : lane_d.shape[1]]
            pieces.append(jnp.where(here, low_d[i * seq : (i + 1) * seq], 0.0))
        low_d = jnp.concatenate(pieces, axis=0).astype(bf16)
        mixed[...] = jnp.dot(hidden[...], wd[...], preferred_element_type=f32) + jnp.dot(
            low_d, downb[...], preferred_element_type=f32
        )
        for i in range(per):
            size = notes[i][pieces_of + 1 : pieces_of + 2, 0:1]
            total = recv[first + i].astype(f32) + mixed[i * seq : (i + 1) * seq, :]
            y[first + i] = jnp.where(row_at < size, total, 0.0).astype(bf16)

        @pl.when(chunk == 0)
        def _():
            each(near, per, lambda p: back_copy(p).start())
            each(0, near, lambda p: back_copy(p).start())

        @pl.when(chunk == 1)
        def _():
            each(per, own, lambda p: back_copy(p).start())
            each(own + 1, groups, lambda p: back_copy(p).start())
            own_back.start()

    def turn(j):
        cols = pl.ds(pl.multiple_of(j * tile_f, tile_f), tile_f)
        turned[cols, :] = jnp.transpose(downa[:, cols].astype(f32)).astype(bf16)

    each(0, units // tile_f, turn)
    each(0, CHUNKS, chunk_step)

    want = lax.broadcasted_iota(jnp.int32, (total_req, slots), 0)

    names = gathered[:, :, :, width:].astype(f32).reshape(slots, 128)
    named = jnp.transpose(names)
    row_id = jnp.where(named[1:2, :] >= 0.0, named[0:1, :] * n_req + named[1:2, :], -1.0)
    place = jnp.where(want == row_id.astype(jnp.int32), 1.0, 0.0).astype(bf16)
    ordered = jnp.dot(place, kept[...], preferred_element_type=f32).astype(bf16)
    lt_ref[...] = lax.dot_general(wh[...], ordered, NT, preferred_element_type=f32)
    slot_id = jnp.where(names[:, 1:2] >= 0.0, names[:, 0:1] * n_req + names[:, 1:2], -1.0)

    def settle(p):
        row_copy(p).wait_send()
        meta_copy(p).wait_send()
        back_copy(p).wait()

    each(0, near, settle)

    def settle_far(p):
        meta_copy(p).wait_send()
        back_copy(p).wait()

    each(near, per, settle_far)
    each(per, own, settle)
    each(own + 1, groups, settle)
    own_back.wait()
    each(1, DEPTH, lambda j: deep_copy(j).wait_send())
    each(0, DEPTH, lambda j: each(1, plane, lambda m: plane_copy(j, m).wait_send()))
    each(0, plane, lambda m: pass_on(m).wait_send())
    each(1, n, lambda k: stat_copy(k).wait())
    tops = stats[:, 0, :]
    best = jnp.max(tops, axis=0, keepdims=True)
    total = jnp.sum(stats[:, 1, :] * jnp.exp(tops - best), axis=0, keepdims=True)
    lse = jnp.transpose(jnp.broadcast_to(best + jnp.log(total), (8, slots)))[:, 0:1]
    across = lax.broadcasted_iota(jnp.int32, (slots, total_req), 1)
    chosen = across == slot_id.astype(jnp.int32)
    lse_ref[...] = jnp.sum(jnp.where(chosen, lse, 0.0), axis=0, keepdims=True)


def finish_kernel(per_dev, ids_hbm, back, lt, lse, out_hbm, lp_hbm, ids, lp, sem, rsem, lsem):
    copy = pltpu.make_async_copy(ids_hbm, ids, sem)
    copy.start()
    shard = lt.shape[0]
    block = pl.cdiv(pl.cdiv(shard, lsem.shape[0]), 8) * 8
    copies = []
    for c, at in enumerate(range(0, shard, block)):
        rows = pl.ds(at, min(block, shard - at))
        lp[rows, :] = lt[rows, :] - lse[...]
        copies.append(pltpu.make_async_copy(lp.at[rows], lp_hbm.at[rows], lsem.at[c]))
        copies[-1].start()
    copy.wait()
    for r in range(out_hbm.shape[0]):
        copies.append(
            pltpu.make_async_copy(
                back.at[lax.div(ids[r], per_dev)], out_hbm.at[r], rsem.at[r]
            )
        )
        copies[-1].start()
    for copy in copies:
        copy.wait()


def finish(per_dev, ids, back, logits_t, lse):
    n_req = ids.shape[0]
    dma = pltpu.SemaphoreType.DMA
    return pl.pallas_call(
        functools.partial(finish_kernel, per_dev),
        out_shape=(
            jax.ShapeDtypeStruct((n_req,) + back.shape[1:], back.dtype),
            jax.ShapeDtypeStruct(logits_t.shape, logits_t.dtype),
        ),
        in_specs=[HBM_SPEC] + [VMEM_SPEC] * 3,
        out_specs=(HBM_SPEC, HBM_SPEC),
        scratch_shapes=[
            pltpu.SMEM((n_req,), jnp.int32),
            pltpu.VMEM(logits_t.shape, logits_t.dtype),
            dma(()), dma((n_req,)), dma((4,)),
        ],
        compiler_params=pltpu.CompilerParams(vmem_limit_bytes=8 << 20),
    )(ids, back, logits_t, lse)


def local(
    residual,
    lengths,
    adapter_ids,
    ffn_gain,
    w_gate_up,
    w_down,
    adapter_input_first,
    ad_out_b,
    ad_down_a,
    adapter_down_second,
    final_gain,
    head_weight,
):
    n_req, seq, width = residual.shape
    groups = lax.axis_size("ad")
    n_q = lax.axis_size("req")
    n = n_q * groups
    per_dev = adapter_input_first.shape[0]
    rank = ad_down_a.shape[1]
    units = w_down.shape[0]
    shard = head_weight.shape[1]
    total_req = n * n_req
    slots = n * groups
    rows = groups // CHUNKS * seq
    plane = n // (2 * DEPTH)
    f32 = jnp.float32
    bf16 = jnp.bfloat16
    ina = adapter_input_first.reshape(per_dev * 2 * rank, width)
    outb = ad_out_b.reshape(per_dev * 2 * rank, units)
    downa = ad_down_a.reshape(per_dev * rank, units)
    downb = adapter_down_second.reshape(per_dev * rank, width)
    head_t = head_weight.T
    dma = pltpu.SemaphoreType.DMA
    vm = pltpu.VMEM
    back, logits_t, lse = pl.pallas_call(
        functools.partial(layer_kernel, n_q, groups, per_dev, n_req),
        out_shape=(
            vm((groups, seq, width), bf16),
            vm((shard, total_req), f32),
            vm((1, total_req), f32),
        ),
        in_specs=[HBM_SPEC] * 12,
        out_specs=(VMEM_SPEC,) * 3,
        scratch_shapes=[
            pltpu.SMEM((n_req,), jnp.int32),
            pltpu.SMEM((n_req,), jnp.int32),
            vm((n_req, seq, width), bf16),
            vm((groups, seq, width), bf16),
            vm((groups, 16, 128), bf16),
            vm((groups, seq, width), bf16),
            vm((groups, 16, 128), bf16),
            vm((rows, width), bf16),
            vm((rows, per_dev * 2 * rank), bf16),
            vm((rows, per_dev * 2 * rank), bf16),
            vm((rows, units), bf16),
            vm((rows, width), f32),
            vm((groups, seq, width), bf16),
            vm((16, 128), f32),
            vm((4, groups, 128), f32),
            vm((groups, width), f32),
            vm((groups, width), bf16),
            vm((groups, units), bf16),
            vm((2, groups, per_dev * 2 * rank), bf16),
            vm(ffn_gain.shape, f32),
            vm(final_gain.shape, f32),
            vm(w_gate_up.shape, bf16),
            vm(w_down.shape, bf16),
            vm(ina.shape, bf16),
            vm(outb.shape, bf16),
            vm(downa.shape, bf16),
            vm(downa.shape[::-1], bf16),
            vm(downb.shape, bf16),
            vm(head_t.shape, bf16),
            vm((n // DEPTH, DEPTH, groups, width + 128), bf16),
            vm((slots, width), bf16),
            vm((n, 2, slots), f32),
            vm((2, slots), f32),
            dma((5,)), dma((12,)), dma(()),
            dma((groups,)), dma((groups,)), dma((groups,)), dma((groups,)),
            dma((groups,)), dma((groups,)),
            dma((DEPTH,)), dma((DEPTH,)),
            dma((DEPTH, plane)), dma((DEPTH, plane)), dma((plane,)), dma((plane,)),
            dma((n,)), dma((n,)),
        ],
        compiler_params=pltpu.CompilerParams(
            collective_id=0, has_side_effects=True, vmem_limit_bytes=60 << 20
        ),
    )(*[
        pltpu.with_memory_space_constraint(v, pltpu.HBM)
        for v in (
            adapter_ids, lengths, residual, ffn_gain, final_gain, w_gate_up, w_down,
            ina, outb, downa, downb, head_t,
        )
    ])
    layer_out, log_probs = finish(per_dev, adapter_ids, back, logits_t, lse)
    return layer_out, log_probs.T


def solution(mesh):
    in_specs = (
        P(("req", "ad"), None, None),
        P(("req", "ad")),
        P(("req", "ad")),
        P(),
        P(),
        P(),
        P("ad", None, None),
        P("ad", None, None, None),
        P("ad", None, None),
        P("ad", None, None),
        P(),
        P(None, ("req", "ad")),
    )
    out_specs = (P(("req", "ad"), None, None), P(None, ("req", "ad")))
    return jax.shard_map(local, mesh=mesh, in_specs=in_specs, out_specs=out_specs, check_vma=False)
```
